32 devices in a mesh: fsdp: 4 (over y, x), ctx: 4 (over z), tp: 2 (over core).
Axes of the slice: x: 2, y: 2, z: 4, core: 2. Of those that a mesh axis runs over, the one named last changes fastest.
Arguments:
- tokens: bfloat16 [8, 2048, 896], P('fsdp', 'ctx'), may hold values from -6 to 6
- cotangent: bfloat16 [8, 2048, 896], P('fsdp', 'ctx'), may hold values from -6 to 6
- segments: int32 [8, 2048], P('fsdp'), may hold values from 0 to 3, as said below
- positions: int32 [8, 2048], P('fsdp', 'ctx'), may hold values from 0 to 2044, as said below
- norm_one: bfloat16 [896], replicated, may hold values from 0.5 to 1.5
- qkv_weight: bfloat16 [896, 2, 576], P(('fsdp', 'ctx'), 'tp'), may hold values from -0.1875 to 0.1875
- qkv_bias: bfloat16 [2, 576], P('tp'), may hold values from -3 to 3
- out_weight: bfloat16 [896, 896], P(('fsdp', 'ctx'), 'tp'), may hold values from -0.75 to 0.75
- norm_two: bfloat16 [896], replicated, may hold values from 0.5 to 1.5
- gate_weight: bfloat16 [896, 4864], P(('fsdp', 'ctx'), 'tp'), may hold values from -0.1875 to 0.1875
- up_weight: bfloat16 [896, 4864], P(('fsdp', 'ctx'), 'tp'), may hold values from -0.1875 to 0.1875
- down_weight: bfloat16 [896, 4864], P(('fsdp', 'ctx'), 'tp'), may hold values from -0.078125 to 0.078125
Outputs:
- block_out: bfloat16 [8, 2048, 896], P('fsdp', ('ctx', 'tp'))
- input_grad: float32 [8, 2048, 896], P('fsdp', 'ctx')
- norm_one_grad: float32 [896], replicated
- qkv_weight_grad: float32 [896, 2, 576], P(('fsdp', 'ctx'), 'tp')
- qkv_bias_grad: float32 [2, 576], P('tp')
- out_weight_grad: float32 [896, 896], P(('fsdp', 'ctx'), 'tp')
- norm_two_grad: float32 [896], replicated
- gate_weight_grad: float32 [896, 4864], P(('fsdp', 'ctx'), 'tp')
- up_weight_grad: float32 [896, 4864], P(('fsdp', 'ctx'), 'tp')
- down_weight_grad: float32 [896, 4864], P(('fsdp', 'ctx'), 'tp')
The draws below stay inside these ranges and needn't reach their ends.
Inputs may be any that keep to these rules, and one draw needn't show every extreme that they name: `segments`: each sequence holds exactly 4 documents, numbered from 0 in order, each a contiguous run; the first token is document 0. `positions`: each token's offset from the first token of its document; the largest is reached in every draw.
All inputs are finite; a program needn't handle non-finite values.
Results may differ from the reference program's by a relative error of at most 0.02.
Values may be sent and summed in bfloat16 or wider, within the bound.
No kernel may reach another device: no remote copies, remote signals or barrier semaphores. Data moves between devices by JAX's collectives and lax.ppermute only.
A program may use at most 256 MiB of HBM per device.

```python
import jax
import jax.numpy as jnp
from jax import lax

D = 896
KV_HEADS = 2
HD = 64
FF = 4864
SEQ_LEN = 2048
DOCS = 4
SEQS = 8
GROUP = 7
QW = 896


def packing(key):
    base_key = jax.random.fold_in(key, 11)
    row_keys = jax.random.split(base_key, SEQS)
    row_numbers = jnp.arange(SEQS, dtype=jnp.int32)

    def one_row(row_key, row_number):
        shuffled = jax.random.permutation(row_key, SEQ_LEN - 1)
        tail_starts = (SEQ_LEN - DOCS + jnp.arange(DOCS - 1, dtype=jnp.int32)).astype(jnp.int32)
        chosen = jnp.where(row_number == 0, tail_starts, shuffled[:DOCS - 1].astype(jnp.int32))
        starts = jnp.zeros((SEQ_LEN,), jnp.int32).at[chosen + 1].set(1).at[0].set(1)
        segment = jnp.cumsum(starts) - 1
        position_index = jnp.arange(SEQ_LEN, dtype=jnp.int32)
        doc_start = lax.cummax(jnp.where(starts == 1, position_index, 0), axis=0)
        return (segment.astype(jnp.int32), (position_index - doc_start).astype(jnp.int32))
    return jax.vmap(one_row)(row_keys, row_numbers)


def draw_segments(key, part):
    return packing(key)[0]


def draw_positions(key, part):
    return packing(key)[1]


def level_of(key, extent, cuts, smallest, top_value):
    level = 1.0
    for dim, shards_of in cuts:
        steps = jax.random.uniform(jax.random.fold_in(jax.random.fold_in(key, 6), dim), (shards_of,), jnp.float32, smallest / len(cuts), top_value / len(cuts))
        level = level * jnp.repeat(jnp.exp(steps), extent[dim] // shards_of).reshape((-1,) + (1,) * (len(extent) - 1 - dim))
    return level


def centred(rng, extent, width, limit, cuts=(), kind=jnp.bfloat16):
    factor_of = level_of(rng, extent, cuts, -0.22, 0.18) if cuts else 1.0
    values = jax.random.normal(rng, extent, jnp.float32) * width * factor_of
    return jnp.minimum(jnp.maximum(values, -limit), limit).astype(kind)


def setup_inputs(seed: int = 0) -> dict:
    keys = jax.random.split(jax.random.key(seed), 13)
    tokens = centred(keys[0], (SEQS, SEQ_LEN, D), 1.0, 6.0, ((0, 4), (1, 4)))
    cotangent = centred(keys[1], (SEQS, SEQ_LEN, D), 1.0, 6.0, ((0, 4), (1, 4)))
    segments = draw_segments(jax.random.fold_in(keys[12], 71), 0)
    positions = draw_positions(jax.random.fold_in(keys[12], 71), 0)
    norm_one = jnp.clip(1.0 + 0.1 * jax.random.normal(keys[4], (D,), jnp.float32), 0.5, 1.5).astype(jnp.bfloat16)
    qkv_weight = centred(keys[5], (D, KV_HEADS, (GROUP + 2) * HD), D ** -0.5, 0.1875, ((0, 16), (1, 2)))
    qkv_bias = centred(keys[6], (KV_HEADS, (GROUP + 2) * HD), 0.5, 3.0, ((0, 2),))
    out_weight = centred(keys[7], (D, QW), HD ** -0.5, 0.75, ((0, 16), (1, 2)))
    norm_two = jnp.clip(1.0 + 0.1 * jax.random.normal(keys[8], (D,), jnp.float32), 0.5, 1.5).astype(jnp.bfloat16)
    gate_weight = centred(keys[9], (D, FF), D ** -0.5, 0.1875, ((0, 16), (1, 2)))
    up_weight = centred(keys[10], (D, FF), D ** -0.5, 0.1875, ((0, 16), (1, 2)))
    down_weight = centred(keys[11], (D, FF), FF ** -0.5, 0.078125, ((0, 16), (1, 2)))
    return dict(tokens=tokens, cotangent=cotangent, segments=segments, positions=positions, norm_one=norm_one, qkv_weight=qkv_weight, qkv_bias=qkv_bias, out_weight=out_weight, norm_two=norm_two, gate_weight=gate_weight, up_weight=up_weight, down_weight=down_weight)


@jax.custom_vjp
def low(v):
    return lax.optimization_barrier(v.astype(jnp.bfloat16)).astype(jnp.float32)

@jax.custom_vjp
def low_back(v):
    return v

def low_keep(v):
    return (low(v), None)

def low_pass(kept, grad):
    return (grad,)

def back_keep(v):
    return (v, None)

def back_low(kept, grad):
    return (low(grad),)
low.defvjp(low_keep, low_pass)
low_back.defvjp(back_keep, back_low)
epsilon = 1e-06
rope_base = 1000000.0
masked_value = -1e+30
highest = lax.Precision.HIGHEST

def rms_norm(values, gain):
    row_scale = lax.rsqrt(lax.optimization_barrier(jnp.mean(values * values, -1, keepdims=True)) + epsilon)
    return values * row_scale * gain

def rotary_tables(positions):
    half_dim = HD // 2
    frequency = rope_base ** (-(jnp.arange(half_dim, dtype=jnp.float32) * 2.0) / HD)
    angles = positions.astype(jnp.float32)[..., None] * frequency
    cosine = jnp.cos(angles)
    sine_table = jnp.sin(angles)
    return (jnp.concatenate([cosine, cosine], -1), jnp.concatenate([sine_table, sine_table], -1))

def rotate(values, cosine, sine_table):
    half_dim = values.shape[-1] // 2
    turned = jnp.concatenate([-values[..., half_dim:], values[..., :half_dim]], -1)
    return values * cosine + turned * sine_table

def attend(pieces):
    query_one, key_one, value_one, segment_one = pieces
    scores = low_back(jnp.einsum('qhgd,khd->hgqk', query_one, key_one, precision=highest) * HD ** (-0.5))
    position_index = jnp.arange(SEQ_LEN)
    allowed = (segment_one[:, None] == segment_one[None, :]) & (position_index[None, :] <= position_index[:, None])
    masked = jnp.where(allowed, scores, masked_value)
    weights = low(jax.nn.softmax(masked, axis=-1))
    return jnp.einsum('hgqk,khd->qhgd', weights, value_one, precision=highest)

def forward(inputs, gain_one, weight_qkv, bias_qkv, weight_out, gain_two, weight_gate, weight_up, weight_down, segments, positions):
    normed = low(rms_norm(inputs, gain_one))
    projected = low_back(jnp.einsum('std,dhc->sthc', normed, weight_qkv, precision=highest) + bias_qkv)
    grouped = projected.reshape(SEQS, SEQ_LEN, KV_HEADS, GROUP + 2, HD)
    cosine, sine_table = rotary_tables(positions)
    queries = low(rotate(grouped[:, :, :, :GROUP], cosine[:, :, None, None], sine_table[:, :, None, None]))
    key_rows = low(rotate(grouped[:, :, :, GROUP], cosine[:, :, None], sine_table[:, :, None]))
    values = low(grouped[:, :, :, GROUP + 1])
    attended = lax.map(jax.checkpoint(attend), (queries, key_rows, values, segments))
    mixed = low(low_back(attended.reshape(SEQS, SEQ_LEN, QW)))
    middle = inputs + low_back(jnp.einsum('stc,dc->std', mixed, weight_out, precision=highest))
    normed_two = low(rms_norm(middle, gain_two))
    gate_act = low_back(jnp.einsum('std,df->stf', normed_two, weight_gate, precision=highest))
    up_act = low_back(jnp.einsum('std,df->stf', normed_two, weight_up, precision=highest))
    hidden = low(jax.nn.silu(gate_act) * up_act)
    return middle + low_back(jnp.einsum('stf,df->std', hidden, weight_down, precision=highest))

def reference(tokens, cotangent, segments, positions, norm_one, qkv_weight, qkv_bias, out_weight, norm_two, gate_weight, up_weight, down_weight):

    def function(inputs, gain_one, weight_qkv, bias_qkv, weight_out, gain_two, weight_gate, weight_up, weight_down):
        return forward(inputs, gain_one, weight_qkv, bias_qkv, weight_out, gain_two, weight_gate, weight_up, weight_down, segments, positions)
    result, pullback = jax.vjp(function, tokens.astype(jnp.float32), norm_one.astype(jnp.float32), qkv_weight.astype(jnp.float32), qkv_bias.astype(jnp.float32), out_weight.astype(jnp.float32), norm_two.astype(jnp.float32), gate_weight.astype(jnp.float32), up_weight.astype(jnp.float32), down_weight.astype(jnp.float32))
    gradients = pullback(cotangent.astype(jnp.float32))
    return (result.astype(jnp.bfloat16), gradients[0], gradients[1], gradients[2], gradients[3], gradients[4], gradients[5], gradients[6], gradients[7], gradients[8])
```

```python
import functools

import jax
import jax.numpy as jnp
from jax import lax
from jax.experimental import pallas as pl
from jax.experimental.pallas import tpu as pltpu
from jax.sharding import PartitionSpec as P

HD = 64
GROUP = 7

epsilon = 1e-06
rope_base = 1000000.0
masked_value = -1e30
contract_rows = (((0,), (0,)), ((), ()))
contract_last = (((1,), (1,)), ((), ()))
contract_first_last = (((0,), (1,)), ((), ()))
f32 = jnp.float32
bf16 = jnp.bfloat16


def mm(a, b, dims=(((1,), (0,)), ((), ()))):
    return lax.dot_general(a, b, dims, preferred_element_type=f32)


def swap_tp(v):
    n = lax.axis_size("tp")
    return lax.ppermute(v, "tp", [(i, (i + 1) % n) for i in range(n)])


def sum_tp(part):
    low = part.astype(bf16)
    return low.astype(f32) + swap_tp(low).astype(f32)


def swap_x(v):
    return lax.ppermute(v, "fsdp", [(i, i ^ 1) for i in range(4)])


def swap_y(v):
    return lax.ppermute(v, "fsdp", [(i, i ^ 2) for i in range(4)])


def ring_up(v):
    n = lax.axis_size("ctx")
    return lax.ppermute(v, "ctx", [(i, (i + 1) % n) for i in range(n)])


def ring_down(v):
    n = lax.axis_size("ctx")
    return lax.ppermute(v, "ctx", [((i + 1) % n, i) for i in range(n)])


def relative_order():
    return lax.axis_size("fsdp") == 4 and lax.axis_size("ctx") % 2 == 0


def gather_rows(w, plane_first=False):
    if not relative_order():
        return lax.all_gather(w, ("fsdp", "ctx"), axis=0, tiled=True)
    steps = lax.axis_size("ctx") - 1
    rows, cols = w.shape
    if plane_first:
        cut = cols // 256 * 128
        x1, y1 = swap_x(w), swap_y(w)
        d1 = jnp.concatenate([swap_y(x1[:, :cut]), swap_x(y1[:, cut:])], 1)
        current = jnp.stack([w, x1, y1, d1])
        pieces = [current]
        for _ in range(steps):
            current = ring_up(current)
            pieces.append(current)
        return jnp.stack(pieces, 1).reshape(-1, cols)
    current = w
    pieces = [w]
    for _ in range(steps):
        current = ring_up(current)
        pieces.append(current)
    own = jnp.concatenate(pieces, 0)
    half = own.shape[0] // 2
    xs, ys = swap_x(own), swap_y(own)
    d1, d2 = swap_y(xs[:half]), swap_x(ys[half:])
    return jnp.concatenate([own, xs, ys, d1, d2], 0)


def add_low(a, b):
    return (a.astype(f32) + b.astype(f32)).astype(bf16)


def scatter_rows(g, plane_first=False):
    if not relative_order():
        return lax.psum_scatter(g, ("fsdp", "ctx"), scatter_dimension=0, tiled=True).astype(f32)
    count = lax.axis_size("ctx")
    cols = g.shape[1]
    g = g.reshape(4, count, -1, cols)
    if plane_first:
        cut = cols // 256 * 128
        total = g[:, count - 1]
        for s in range(count - 2, -1, -1):
            total = add_low(ring_down(total), g[:, s])
        own, gx, gy, gd = (total[i] for i in range(4))
        r1, r2 = swap_y(gd[:, :cut]), swap_x(gd[:, cut:])
        gx = jnp.concatenate([add_low(gx[:, :cut], r1), gx[:, cut:]], 1)
        gy = jnp.concatenate([gy[:, :cut], add_low(gy[:, cut:], r2)], 1)
        return own.astype(f32) + swap_x(gx).astype(f32) + swap_y(gy).astype(f32)
    half = count // 2
    own, gx, gy, gd = (g[i] for i in range(4))
    r1, r2 = swap_y(gd[:half]), swap_x(gd[half:])
    gx = jnp.concatenate([add_low(gx[:half], r1), gx[half:]], 0)
    gy = jnp.concatenate([gy[:half], add_low(gy[half:], r2)], 0)
    plane = (own.astype(f32) + swap_x(gx).astype(f32) + swap_y(gy).astype(f32)).astype(bf16)
    total = plane[count - 1]
    for s in range(count - 2, 0, -1):
        total = add_low(ring_down(total), plane[s])
    return ring_down(total).astype(f32) + plane[0].astype(f32)


def order_matrix(model_width):
    if not relative_order():
        return None
    count = lax.axis_size("ctx")
    rows = model_width // (4 * count)
    place = jnp.arange(model_width, dtype=jnp.int32)
    block = place // rows
    fsdp = lax.axis_index("fsdp") ^ (block // count)
    ctx = (lax.axis_index("ctx") - block % count + count) % count
    source = (fsdp * count + ctx) * rows + place % rows
    return (jnp.arange(model_width, dtype=jnp.int32)[:, None] == source[None, :]).astype(bf16)


def to_relative(v, order):
    return v if order is None else mm(v, order).astype(v.dtype)


def to_canonical(v, order):
    return v if order is None else mm(v, order, contract_last).astype(v.dtype)


def allowed_pairs(pos, offset, keys, block):
    gap = (
        lax.broadcasted_iota(jnp.int32, (keys, block), 1)
        - lax.broadcasted_iota(jnp.int32, (keys, block), 0)
        + offset
    )
    return (gap >= 0) & (gap <= pos)


def attend_kernel(count_ref, q_ref, pos_ref, kv_ref, vt_ref, o_ref, lse_ref, m_ref, l_ref, acc_ref):
    block = q_ref.shape[1]
    pos = pos_ref[0]
    m_ref[...] = jnp.full(m_ref.shape, masked_value, f32)
    l_ref[...] = jnp.zeros(l_ref.shape, f32)
    acc_ref[...] = jnp.zeros(acc_ref.shape, f32)

    def step(s, carry):
        keep = allowed_pairs(pos, s * block, block, block)
        keys = kv_ref[0, s, :, :HD]
        values_t = vt_ref[0, s]
        for g in range(GROUP):
            rows = slice(g * HD, (g + 1) * HD)
            scores = jnp.where(keep, mm(keys, q_ref[rows, :]), masked_value)
            old = m_ref[g : g + 1, :]
            top = jnp.maximum(old, jnp.max(scores, 0, keepdims=True))
            weight = jnp.exp(scores - top)
            shrink = jnp.exp(old - top)
            m_ref[g : g + 1, :] = top
            l_ref[g : g + 1, :] = l_ref[g : g + 1, :] * shrink + jnp.sum(weight, 0, keepdims=True)
            acc_ref[rows, :] = acc_ref[rows, :] * shrink + mm(values_t, weight.astype(bf16))
        return carry

    lax.fori_loop(0, count_ref[pl.program_id(0)], step, 0)
    for g in range(GROUP):
        rows = slice(g * HD, (g + 1) * HD)
        total = l_ref[g : g + 1, :]
        o_ref[rows, :] = (acc_ref[rows, :] / total).astype(bf16)
        lse_ref[0, g : g + 1, :] = m_ref[g : g + 1, :] + jnp.log(total)
    lse_ref[0, GROUP : GROUP + 1, :] = jnp.zeros((1, block), f32)


def attend_back_kernel(
    count_ref, q_ref, pos_ref, kv_ref, kt_ref, o_ref, lse_ref, do_ref, dq_ref, dkv_ref, dq_acc
):
    block = q_ref.shape[1]
    pos = pos_ref[0]
    dkv_ref[...] = jnp.zeros(dkv_ref.shape, bf16)
    dq_acc[...] = jnp.zeros(dq_acc.shape, f32)

    def step(s, carry):
        keep = allowed_pairs(pos, s * block, block, block)
        keys = kv_ref[0, s, :, :HD]
        values = kv_ref[0, s, :, HD:]
        keys_t = kt_ref[0, s]
        key_grad = jnp.zeros((block, HD), f32)
        value_grad = jnp.zeros((block, HD), f32)
        for g in range(GROUP):
            rows = slice(g * HD, (g + 1) * HD)
            query = q_ref[rows, :]
            grad = do_ref[rows, :]
            centre = jnp.sum(grad.astype(f32) * o_ref[rows, :].astype(f32), 0, keepdims=True)
            scores = mm(keys, query) - lse_ref[0, g : g + 1, :]
            probs = jnp.exp(jnp.where(keep, scores, masked_value))
            prob_grad = mm(values, grad)
            score_grad = (probs * (prob_grad - centre)).astype(bf16)
            value_grad = value_grad + mm(probs.astype(bf16), grad, contract_last)
            key_grad = key_grad + mm(score_grad, query, contract_last)
            dq_acc[rows, :] += mm(keys_t, score_grad)
        dkv_ref[0, s, :, :HD] = key_grad.astype(bf16)
        dkv_ref[0, s, :, HD:] = value_grad.astype(bf16)
        return carry

    lax.fori_loop(0, count_ref[pl.program_id(0)], step, 0)
    dq_ref[...] = dq_acc[...] * HD ** (-0.5)


def attention_specs(block, count):
    return dict(
        wide=pl.BlockSpec((GROUP * HD, block), lambda i, *_: (0, i)),
        pos=pl.BlockSpec((1, 1, block), lambda i, *_: (i, 0, 0)),
        kv=pl.BlockSpec((1, count, block, 2 * HD), lambda i, *_: (i, 0, 0, 0)),
        half=pl.BlockSpec((1, count, HD, block), lambda i, *_: (i, 0, 0, 0)),
        lse=pl.BlockSpec((1, GROUP + 1, block), lambda i, *_: (i, 0, 0)),
    )


VMEM_BYTES = 48 * 1024 * 1024


def attend(counts, queries, pos, kv, values_t, block):
    seqs, count = kv.shape[:2]
    spec = attention_specs(block, count)
    work = seqs * GROUP * block * block * count
    return pl.pallas_call(
        attend_kernel,
        grid_spec=pltpu.PrefetchScalarGridSpec(
            num_scalar_prefetch=1,
            grid=(seqs,),
            in_specs=[spec["wide"], spec["pos"], spec["kv"], spec["half"]],
            out_specs=[spec["wide"], spec["lse"]],
            scratch_shapes=[
                pltpu.VMEM((GROUP + 1, block), f32),
                pltpu.VMEM((GROUP + 1, block), f32),
                pltpu.VMEM((GROUP * HD, block), f32),
            ],
        ),
        out_shape=[
            jax.ShapeDtypeStruct((GROUP * HD, seqs * block), bf16),
            jax.ShapeDtypeStruct((seqs, GROUP + 1, block), f32),
        ],
        compiler_params=pltpu.CompilerParams(vmem_limit_bytes=VMEM_BYTES),
        cost_estimate=pl.CostEstimate(
            flops=4 * HD * work * 4, bytes_accessed=4 * 1024 * 1024, transcendentals=work
        ),
        name="attend",
    )(counts, queries, pos, kv, values_t)


def attend_back(counts, queries, pos, kv, keys_t, mixed, lse, mixed_grad, block):
    seqs, count = kv.shape[:2]
    spec = attention_specs(block, count)
    work = seqs * GROUP * block * block * count
    return pl.pallas_call(
        attend_back_kernel,
        grid_spec=pltpu.PrefetchScalarGridSpec(
            num_scalar_prefetch=1,
            grid=(seqs,),
            in_specs=[
                spec["wide"], spec["pos"], spec["kv"], spec["half"],
                spec["wide"], spec["lse"], spec["wide"],
            ],
            out_specs=[spec["wide"], spec["kv"]],
            scratch_shapes=[pltpu.VMEM((GROUP * HD, block), f32)],
        ),
        out_shape=[
            jax.ShapeDtypeStruct((GROUP * HD, seqs * block), f32),
            jax.ShapeDtypeStruct((seqs, count, block, 2 * HD), bf16),
        ],
        compiler_params=pltpu.CompilerParams(vmem_limit_bytes=VMEM_BYTES),
        cost_estimate=pl.CostEstimate(
            flops=10 * HD * work * 4, bytes_accessed=8 * 1024 * 1024, transcendentals=work
        ),
        name="attend_back",
    )(counts, queries, pos, kv, keys_t, mixed, lse, mixed_grad)


def rotate_rows(v, cosine, sine):
    half = HD // 2
    low, high = v[:, :half], v[:, half:]
    return jnp.concatenate([low * cosine - high * sine, high * cosine + low * sine], 1)


def feed_parts(width):
    tiles = width // 128
    if width % 128 or tiles < 4:
        return [(0, width)]
    each = -(-tiles // 4)
    ends = [0, each * 128, 2 * each * 128, 3 * each * 128, width]
    return [(a, b) for a, b in zip(ends[:-1], ends[1:]) if b > a]


def shards(
    tokens,
    cotangent,
    segments,
    positions,
    norm_one,
    qkv_weight,
    qkv_bias,
    out_weight,
    norm_two,
    gate_weight,
    up_weight,
    down_weight,
):
    del segments
    seqs, block, width = tokens.shape
    rows = seqs * block
    per_group = qkv_weight.shape[2]
    q_width = out_weight.shape[1]
    count = lax.axis_size("ctx")
    tp = lax.axis_size("tp")
    half_len = block // tp
    half_start = lax.axis_index("tp") * half_len

    pack_low = jnp.concatenate([qkv_weight[:, 0], out_weight], 1)
    attention_full = gather_rows(pack_low)
    qkv_full = attention_full[:, :per_group]
    out_full = attention_full[:, per_group:]
    parts = feed_parts(gate_weight.shape[1])
    feed_full = []
    for i, (a, b) in enumerate(parts):
        own = jnp.concatenate([gate_weight[:, a:b], up_weight[:, a:b], down_weight[:, a:b]], 1)
        feed_full.append(gather_rows(own, i == len(parts) - 1 and len(parts) > 1))

    order = order_matrix(width)
    x_low = to_relative(tokens.reshape(rows, width), order)
    upstream_low = to_relative(cotangent.reshape(rows, width), order)
    gains = to_relative(jnp.stack([norm_one, norm_two]), order).astype(f32)
    gain_one, gain_two = gains[0:1], gains[1:2]

    inputs = x_low.astype(f32)
    scale_one = lax.rsqrt(jnp.mean(inputs * inputs, -1, keepdims=True) + epsilon)
    unit_one = inputs * scale_one
    normed = (unit_one * gain_one).astype(bf16)

    projected = mm(qkv_full, normed, contract_first_last) + qkv_bias[0].astype(f32)[:, None]
    frequency = rope_base ** (-(jnp.arange(HD // 2, dtype=f32) * 2.0) / HD)
    angles = positions.reshape(1, rows).astype(f32) * frequency[:, None]
    cosine, sine = jnp.cos(angles), jnp.sin(angles)
    turned = rotate_rows(
        projected[: (GROUP + 1) * HD].reshape(GROUP + 1, HD, rows), cosine, sine
    )
    queries = (turned[:GROUP] * HD ** (-0.5)).astype(bf16).reshape(GROUP * HD, rows)
    kv_t = jnp.concatenate([turned[GROUP], projected[(GROUP + 1) * HD :]], 0).astype(bf16)
    kv_own = kv_t.T.reshape(seqs, block, 2 * HD)
    kv_blocks = [kv_own]
    for s in range(1, count):
        kv_blocks.append(lax.ppermute(kv_own, "ctx", [(i, i + s) for i in range(count - s)]))
    kv = jnp.stack(kv_blocks, 1)
    kv_turned = jnp.swapaxes(kv, 2, 3)
    keys_t, values_t = kv_turned[:, :, :HD], kv_turned[:, :, HD:]
    place = jnp.arange(block, dtype=jnp.int32)
    reach = jnp.max(positions - place[None], 1)
    counts = 1 + jnp.minimum((jnp.maximum(reach, 0) + block - 1) // block, lax.axis_index("ctx"))
    counts = counts.astype(jnp.int32)
    pos = positions.reshape(seqs, 1, block)

    mixed, lse = attend(counts, queries, pos, kv, values_t, block)
    branch = sum_tp(mm(mixed, out_full, contract_first_last))
    middle = inputs + branch
    scale_two = lax.rsqrt(jnp.mean(middle * middle, -1, keepdims=True) + epsilon)
    unit_two = middle * scale_two
    normed_two = (unit_two * gain_two).astype(bf16)

    feed_out = jnp.zeros((rows, width), f32)
    normed_two_part = jnp.zeros((rows, width), f32)
    feed_grads = []
    for i, ((a, b), full) in enumerate(zip(parts, feed_full)):
        c = b - a
        gate_w, up_w, down_w = full[:, :c], full[:, c : 2 * c], full[:, 2 * c :]
        gate_act = mm(normed_two, gate_w)
        up_act = mm(normed_two, up_w)
        hidden_grad = mm(upstream_low, down_w)
        sigmoid = jax.nn.sigmoid(gate_act)
        silu_gate = gate_act * sigmoid
        hidden = (silu_gate * up_act).astype(bf16)
        gate_grad = (hidden_grad * up_act * (sigmoid * (1.0 + gate_act * (1.0 - sigmoid)))).astype(bf16)
        up_grad = (hidden_grad * silu_gate).astype(bf16)
        feed_out = feed_out + mm(hidden, down_w, contract_last)
        normed_two_part = (
            normed_two_part + mm(gate_grad, gate_w, contract_last) + mm(up_grad, up_w, contract_last)
        )
        grads = jnp.concatenate(
            [
                mm(normed_two, gate_grad, contract_rows).astype(bf16),
                mm(normed_two, up_grad, contract_rows).astype(bf16),
                mm(upstream_low, hidden, contract_rows).astype(bf16),
            ],
            1,
        )
        total = scatter_rows(grads, i == len(parts) - 1 and len(parts) > 1)
        feed_grads.append((total[:, :c], total[:, c : 2 * c], total[:, 2 * c :]))
    feed_grads = [jnp.concatenate([p[j] for p in feed_grads], 1) for j in range(3)]

    feed_low = feed_out.astype(bf16).reshape(seqs, block, width)

    def own_rows(v, start):
        return lax.dynamic_slice_in_dim(v, start, half_len, 1)

    other_start = (half_len * (tp - 1) - half_start) if tp == 2 else None
    feed_other = swap_tp(own_rows(feed_low, other_start))
    feed_sum = own_rows(feed_low, half_start).astype(f32) + feed_other.astype(f32)
    block_low = (own_rows(middle.reshape(seqs, block, width), half_start) + feed_sum).astype(bf16)
    block_out = to_canonical(block_low.reshape(-1, width), order).reshape(seqs, half_len, width)

    normed_two_grad = sum_tp(normed_two_part)
    gain_two_grad = jnp.sum(normed_two_grad * unit_two, 0, keepdims=True)
    scaled_two = normed_two_grad * gain_two
    middle_grad = upstream_low.astype(f32) + scale_two * (
        scaled_two - unit_two * jnp.mean(scaled_two * unit_two, -1, keepdims=True)
    )
    branch_low = middle_grad.astype(bf16)
    mixed_grad = mm(out_full, branch_low, contract_first_last).astype(bf16)
    out_weight_grad = mm(branch_low, mixed, contract_first_last_rows).astype(bf16)

    query_grads, pack_grads = attend_back(
        counts, queries, pos, kv, keys_t, mixed, lse, mixed_grad, block
    )
    pack_sum = pack_grads[:, 0].astype(f32)
    for s in range(1, count):
        pack_sum = pack_sum + lax.ppermute(
            pack_grads[:, s], "ctx", [(i + s, i) for i in range(count - s)]
        ).astype(f32)
    pack_t = pack_sum.reshape(rows, 2 * HD).T
    grouped = jnp.concatenate([query_grads, pack_t[:HD]], 0).reshape(GROUP + 1, HD, rows)
    turned_back = rotate_rows(grouped, cosine, -sine).reshape((GROUP + 1) * HD, rows)
    projected_grad = jnp.concatenate([turned_back, pack_t[HD:]], 0).astype(bf16)
    bias_grad = jnp.sum(projected_grad.astype(f32), 1)[None]
    qkv_weight_grad = mm(normed, projected_grad, contract_first_last_rows).astype(bf16)
    attention_total = scatter_rows(jnp.concatenate([qkv_weight_grad, out_weight_grad], 1))

    normed_one_grad = sum_tp(mm(projected_grad, qkv_full, contract_first_last))
    gain_one_grad = jnp.sum(normed_one_grad * unit_one, 0, keepdims=True)
    scaled_one = normed_one_grad * gain_one
    input_grad = middle_grad + scale_one * (
        scaled_one - unit_one * jnp.mean(scaled_one * unit_one, -1, keepdims=True)
    )
    input_grad = to_canonical(input_grad.astype(bf16), order).astype(f32)
    gain_grads = jnp.concatenate([gain_one_grad, gain_two_grad], 0)
    if order is not None:
        gain_grads = lax.dot_general(
            gain_grads, order.astype(f32), contract_last, precision=lax.Precision.HIGHEST
        )
    gain_total, bias_total = lax.psum((gain_grads, bias_grad), ("fsdp", "ctx"))
    return (
        block_out,
        input_grad.reshape(seqs, block, width),
        gain_total[0],
        attention_total[:, :per_group][:, None, :],
        bias_total,
        attention_total[:, per_group:],
        gain_total[1],
        feed_grads[0],
        feed_grads[1],
        feed_grads[2],
    )


contract_first_last_rows = (((0,), (1,)), ((), ()))


def solution(mesh):
    weight = P(("fsdp", "ctx"), "tp")
    return jax.shard_map(
        shards,
        mesh=mesh,
        in_specs=(
            P("fsdp", "ctx", None),
            P("fsdp", "ctx", None),
            P("fsdp", None),
            P("fsdp", "ctx"),
            P(),
            P(("fsdp", "ctx"), "tp", None),
            P("tp", None),
            weight,
            P(),
            weight,
            weight,
            weight,
        ),
        out_specs=(
            P("fsdp", ("ctx", "tp"), None),
            P("fsdp", "ctx", None),
            P(),
            P(("fsdp", "ctx"), "tp", None),
            P("tp", None),
            weight,
            P(),
            weight,
            weight,
            weight,
        ),
        check_vma=False,
    )
```

```python
import functools

import jax
import jax.numpy as jnp
from jax import lax
from jax.experimental import pallas as pl
from jax.experimental.pallas import tpu as pltpu
from jax.sharding import PartitionSpec as P

HD = 64
GROUP = 7

epsilon = 1e-06
rope_base = 1000000.0
masked_value = -1e30
contract_rows = (((0,), (0,)), ((), ()))
contract_last = (((1,), (1,)), ((), ()))
contract_first_last = (((0,), (1,)), ((), ()))
f32 = jnp.float32
bf16 = jnp.bfloat16


def mm(a, b, dims=(((1,), (0,)), ((), ()))):
    return lax.dot_general(a, b, dims, preferred_element_type=f32)


def swap_tp(v):
    n = lax.axis_size("tp")
    return lax.ppermute(v, "tp", [(i, (i + 1) % n) for i in range(n)])


def sum_tp(part):
    low = part.astype(bf16)
    return low.astype(f32) + swap_tp(low).astype(f32)


def swap_x(v):
    return lax.ppermute(v, "fsdp", [(i, i ^ 1) for i in range(4)])


def swap_y(v):
    return lax.ppermute(v, "fsdp", [(i, i ^ 2) for i in range(4)])


def ring_up(v):
    n = lax.axis_size("ctx")
    return lax.ppermute(v, "ctx", [(i, (i + 1) % n) for i in range(n)])


def ring_down(v):
    n = lax.axis_size("ctx")
    return lax.ppermute(v, "ctx", [((i + 1) % n, i) for i in range(n)])


def swap_xy(v):
    return lax.ppermute(v, "fsdp", [(i, i ^ 3) for i in range(4)])


def sum_all(v):
    for axis in ("fsdp", "ctx"):
        n = lax.axis_size(axis)
        if n & (n - 1):
            v = lax.psum(v, axis)
            continue
        step = 1
        while step < n:
            v = v + lax.ppermute(v, axis, [(i, i ^ step) for i in range(n)])
            step *= 2
    return v


def relative_order():
    return lax.axis_size("fsdp") == 4 and lax.axis_size("ctx") % 2 == 0


def ring_pieces(w):
    pieces = [w]
    for _ in range(lax.axis_size("ctx") - 1):
        pieces.append(ring_up(pieces[-1]))
    return pieces


def gather_plane(w):
    if not relative_order():
        return [lax.all_gather(w, ("fsdp", "ctx"), axis=0, tiled=True)]
    own = jnp.concatenate(ring_pieces(w), 0)
    half = own.shape[0] // 2
    xs, ys = swap_x(own), swap_y(own)
    return [own, xs, ys, swap_y(xs[:half]), swap_x(ys[half:])]


def gather_line(w):
    if not relative_order():
        return [lax.all_gather(w, ("fsdp", "ctx"), axis=0, tiled=True)]
    cols = w.shape[1]
    pieces = ring_pieces(jnp.concatenate([w, swap_xy(w)], 1))
    own = jnp.concatenate([p[:, :cols] for p in pieces], 0)
    far = jnp.concatenate([p[:, cols:] for p in pieces], 0)
    return [own, swap_x(own), swap_y(own), far]


def add_low(*terms):
    return sum(t.astype(f32) for t in terms).astype(bf16)


def ring_sum(v, last=f32):
    total = v[-1]
    for s in range(v.shape[0] - 2, 0, -1):
        total = add_low(ring_down(total), v[s])
    return ring_down(total).astype(f32) + v[0].astype(f32)


def scatter_plane(pieces):
    if not relative_order():
        return lax.psum_scatter(
            pieces[0], ("fsdp", "ctx"), scatter_dimension=0, tiled=True
        ).astype(f32)
    count = lax.axis_size("ctx")
    own, gx, gy, g1, g2 = pieces
    half = own.shape[0] // 2
    r1, r2 = swap_y(g1), swap_x(g2)
    gx = jnp.concatenate([add_low(gx[:half], r1), gx[half:]], 0)
    gy = jnp.concatenate([gy[:half], add_low(gy[half:], r2)], 0)
    plane = add_low(own, swap_x(gx), swap_y(gy))
    return ring_sum(plane.reshape(count, -1, own.shape[1]))


def scatter_line(pieces):
    if not relative_order():
        return lax.psum_scatter(
            pieces[0], ("fsdp", "ctx"), scatter_dimension=0, tiled=True
        ).astype(f32)
    count = lax.axis_size("ctx")
    own, gx, gy, far = pieces
    cols = own.shape[1]
    plane = add_low(own, swap_x(gx), swap_y(gy))
    both = jnp.concatenate([plane, far], 1).reshape(count, -1, 2 * cols)
    total = ring_sum(both)
    return total[:, :cols] + swap_xy(total[:, cols:].astype(bf16)).astype(f32)


def row_pieces(g):
    if not relative_order():
        return [g]
    part = g.shape[0] // 8
    ends = [0, 2 * part, 4 * part, 6 * part, 7 * part, 8 * part]
    return [g[a:b] for a, b in zip(ends[:-1], ends[1:])]


def order_matrix(model_width):
    if not relative_order():
        return None
    count = lax.axis_size("ctx")
    rows = model_width // (4 * count)
    place = jnp.arange(model_width, dtype=jnp.int32)
    block = place // rows
    fsdp = lax.axis_index("fsdp") ^ (block // count)
    ctx = (lax.axis_index("ctx") - block % count + count) % count
    source = (fsdp * count + ctx) * rows + place % rows
    return (jnp.arange(model_width, dtype=jnp.int32)[:, None] == source[None, :]).astype(bf16)


def to_relative(v, order):
    return v if order is None else mm(v, order).astype(v.dtype)


def to_canonical(v, order):
    return v if order is None else mm(v, order, contract_last).astype(v.dtype)


def allowed_pairs(pos, offset, keys, block):
    gap = (
        lax.broadcasted_iota(jnp.int32, (keys, block), 1)
        - lax.broadcasted_iota(jnp.int32, (keys, block), 0)
        + offset
    )
    return (gap >= 0) & (gap <= pos)


def attend_kernel(count_ref, q_ref, pos_ref, kv_ref, vt_ref, o_ref, lse_ref, m_ref, l_ref, acc_ref):
    block = q_ref.shape[1]
    pos = pos_ref[0]
    m_ref[...] = jnp.full(m_ref.shape, masked_value, f32)
    l_ref[...] = jnp.zeros(l_ref.shape, f32)
    acc_ref[...] = jnp.zeros(acc_ref.shape, f32)

    def step(s, carry):
        keep = allowed_pairs(pos, s * block, block, block)
        keys = kv_ref[0, s, :, :HD]
        values_t = vt_ref[0, s]
        for g in range(GROUP):
            rows = slice(g * HD, (g + 1) * HD)
            scores = jnp.where(keep, mm(keys, q_ref[rows, :]), masked_value)
            old = m_ref[g : g + 1, :]
            top = jnp.maximum(old, jnp.max(scores, 0, keepdims=True))
            weight = jnp.exp(scores - top)
            shrink = jnp.exp(old - top)
            m_ref[g : g + 1, :] = top
            l_ref[g : g + 1, :] = l_ref[g : g + 1, :] * shrink + jnp.sum(weight, 0, keepdims=True)
            acc_ref[rows, :] = acc_ref[rows, :] * shrink + mm(values_t, weight.astype(bf16))
        return carry

    lax.fori_loop(0, count_ref[pl.program_id(0)], step, 0)
    for g in range(GROUP):
        rows = slice(g * HD, (g + 1) * HD)
        total = l_ref[g : g + 1, :]
        o_ref[rows, :] = (acc_ref[rows, :] / total).astype(bf16)
        lse_ref[0, g : g + 1, :] = m_ref[g : g + 1, :] + jnp.log(total)
    lse_ref[0, GROUP : GROUP + 1, :] = jnp.zeros((1, block), f32)


def attend_back_kernel(
    count_ref, q_ref, pos_ref, kv_ref, kt_ref, o_ref, lse_ref, do_ref, dq_ref, dkv_ref, dq_acc
):
    block = q_ref.shape[1]
    pos = pos_ref[0]
    dkv_ref[...] = jnp.zeros(dkv_ref.shape, bf16)
    dq_acc[...] = jnp.zeros(dq_acc.shape, f32)

    def step(s, carry):
        keep = allowed_pairs(pos, s * block, block, block)
        keys = kv_ref[0, s, :, :HD]
        values = kv_ref[0, s, :, HD:]
        keys_t = kt_ref[0, s]
        key_grad = jnp.zeros((block, HD), f32)
        value_grad = jnp.zeros((block, HD), f32)
        for g in range(GROUP):
            rows = slice(g * HD, (g + 1) * HD)
            query = q_ref[rows, :]
            grad = do_ref[rows, :]
            centre = jnp.sum(grad.astype(f32) * o_ref[rows, :].astype(f32), 0, keepdims=True)
            scores = mm(keys, query) - lse_ref[0, g : g + 1, :]
            probs = jnp.exp(jnp.where(keep, scores, masked_value))
            prob_grad = mm(values, grad)
            score_grad = (probs * (prob_grad - centre)).astype(bf16)
            value_grad = value_grad + mm(probs.astype(bf16), grad, contract_last)
            key_grad = key_grad + mm(score_grad, query, contract_last)
            dq_acc[rows, :] += mm(keys_t, score_grad)
        dkv_ref[0, s, :, :HD] = key_grad.astype(bf16)
        dkv_ref[0, s, :, HD:] = value_grad.astype(bf16)
        return carry

    lax.fori_loop(0, count_ref[pl.program_id(0)], step, 0)
    dq_ref[...] = dq_acc[...] * HD ** (-0.5)


def attention_specs(block, count):
    return dict(
        wide=pl.BlockSpec((GROUP * HD, block), lambda i, *_: (0, i)),
        pos=pl.BlockSpec((1, 1, block), lambda i, *_: (i, 0, 0)),
        kv=pl.BlockSpec((1, count, block, 2 * HD), lambda i, *_: (i, 0, 0, 0)),
        half=pl.BlockSpec((1, count, HD, block), lambda i, *_: (i, 0, 0, 0)),
        lse=pl.BlockSpec((1, GROUP + 1, block), lambda i, *_: (i, 0, 0)),
    )


VMEM_BYTES = 48 * 1024 * 1024


def attend(counts, queries, pos, kv, values_t, block):
    seqs, count = kv.shape[:2]
    spec = attention_specs(block, count)
    work = seqs * GROUP * block * block * count
    return pl.pallas_call(
        attend_kernel,
        grid_spec=pltpu.PrefetchScalarGridSpec(
            num_scalar_prefetch=1,
            grid=(seqs,),
            in_specs=[spec["wide"], spec["pos"], spec["kv"], spec["half"]],
            out_specs=[spec["wide"], spec["lse"]],
            scratch_shapes=[
                pltpu.VMEM((GROUP + 1, block), f32),
                pltpu.VMEM((GROUP + 1, block), f32),
                pltpu.VMEM((GROUP * HD, block), f32),
            ],
        ),
        out_shape=[
            jax.ShapeDtypeStruct((GROUP * HD, seqs * block), bf16),
            jax.ShapeDtypeStruct((seqs, GROUP + 1, block), f32),
        ],
        compiler_params=pltpu.CompilerParams(vmem_limit_bytes=VMEM_BYTES),
        cost_estimate=pl.CostEstimate(
            flops=4 * HD * work * 4, bytes_accessed=4 * 1024 * 1024, transcendentals=work
        ),
        name="attend",
    )(counts, queries, pos, kv, values_t)


def attend_back(counts, queries, pos, kv, keys_t, mixed, lse, mixed_grad, block):
    seqs, count = kv.shape[:2]
    spec = attention_specs(block, count)
    work = seqs * GROUP * block * block * count
    return pl.pallas_call(
        attend_back_kernel,
        grid_spec=pltpu.PrefetchScalarGridSpec(
            num_scalar_prefetch=1,
            grid=(seqs,),
            in_specs=[
                spec["wide"], spec["pos"], spec["kv"], spec["half"],
                spec["wide"], spec["lse"], spec["wide"],
            ],
            out_specs=[spec["wide"], spec["kv"]],
            scratch_shapes=[pltpu.VMEM((GROUP * HD, block), f32)],
        ),
        out_shape=[
            jax.ShapeDtypeStruct((GROUP * HD, seqs * block), f32),
            jax.ShapeDtypeStruct((seqs, count, block, 2 * HD), bf16),
        ],
        compiler_params=pltpu.CompilerParams(vmem_limit_bytes=VMEM_BYTES),
        cost_estimate=pl.CostEstimate(
            flops=10 * HD * work * 4, bytes_accessed=8 * 1024 * 1024, transcendentals=work
        ),
        name="attend_back",
    )(counts, queries, pos, kv, keys_t, mixed, lse, mixed_grad)


def feed_kernel(starts, width, tile, *refs):
    k = len(starts)
    n_ref, c_ref = refs[:2]
    w_refs = refs[2 : 2 + k]
    out_ref, dn_ref = refs[2 + k : 4 + k]
    g_refs = refs[4 + k : 4 + 2 * k]
    gate_up, down, n_t, c_t, hidden_s, pair_s, out_acc, dn_acc = refs[4 + 2 * k :]
    step = pl.program_id(0)

    @pl.when(step == 0)
    def _():
        n_t[...] = n_ref[...].T
        c_t[...] = c_ref[...].T
        out_acc[...] = jnp.zeros(out_acc.shape, f32)
        dn_acc[...] = jnp.zeros(dn_acc.shape, f32)

    for start, w_ref in zip(starts, w_refs):
        rows = slice(start, start + w_ref.shape[0])
        gate_up[rows, :] = w_ref[:, : 2 * width]
        down[rows, :] = w_ref[:, 2 * width :]

    def token_tile(t, carry):
        rows = pl.ds(pl.multiple_of(t * tile, tile), tile)
        both = mm(n_ref[rows, :], gate_up[...])
        hidden_grad = mm(c_ref[rows, :], down[...])
        gate, up = both[:, :width], both[:, width:]
        sigmoid = jax.nn.sigmoid(gate)
        silu = gate * sigmoid
        hidden = (silu * up).astype(bf16)
        gate_grad = hidden_grad * up * (sigmoid * (1.0 + gate * (1.0 - sigmoid)))
        pair = jnp.concatenate([gate_grad.astype(bf16), (hidden_grad * silu).astype(bf16)], 1)
        hidden_s[rows, :] = hidden
        pair_s[rows, :] = pair
        out_acc[rows, :] += mm(hidden, down[...], contract_last)
        dn_acc[rows, :] += mm(pair, gate_up[...], contract_last)
        return carry

    lax.fori_loop(0, n_ref.shape[0] // tile, token_tile, 0)
    pair_grad = mm(n_t[...], pair_s[...]).astype(bf16)
    down_grad = mm(c_t[...], hidden_s[...]).astype(bf16)
    for start, g_ref in zip(starts, g_refs):
        rows = slice(start, start + g_ref.shape[0])
        g_ref[:, : 2 * width] = pair_grad[rows]
        g_ref[:, 2 * width :] = down_grad[rows]

    @pl.when(step == pl.num_programs(0) - 1)
    def _():
        out_ref[...] = out_acc[...].astype(bf16)
        dn_ref[...] = dn_acc[...].astype(bf16)


def feed_group(normed, upstream, pieces, width):
    rows, model = normed.shape
    chunks = pieces[0].shape[1] // (3 * width)
    starts, start = [], 0
    for p in pieces:
        starts.append(start)
        start += p.shape[0]
    tile = min(rows, 256)
    whole = pl.BlockSpec((rows, model), lambda j: (0, 0))
    blocks = [pl.BlockSpec((p.shape[0], 3 * width), lambda j: (0, j)) for p in pieces]
    hidden = chunks * width
    return pl.pallas_call(
        functools.partial(feed_kernel, starts, width, tile),
        grid=(chunks,),
        in_specs=[whole, whole] + blocks,
        out_specs=[whole, whole] + blocks,
        out_shape=[jax.ShapeDtypeStruct((rows, model), bf16)] * 2
        + [jax.ShapeDtypeStruct(p.shape, bf16) for p in pieces],
        scratch_shapes=[
            pltpu.VMEM((model, 2 * width), bf16),
            pltpu.VMEM((model, width), bf16),
            pltpu.VMEM((model, rows), bf16),
            pltpu.VMEM((model, rows), bf16),
            pltpu.VMEM((rows, width), bf16),
            pltpu.VMEM((rows, 2 * width), bf16),
            pltpu.VMEM((rows, model), f32),
            pltpu.VMEM((rows, model), f32),
        ],
        compiler_params=pltpu.CompilerParams(vmem_limit_bytes=VMEM_BYTES),
        cost_estimate=pl.CostEstimate(
            flops=18 * rows * model * hidden,
            bytes_accessed=12 * model * hidden + 8 * rows * model,
            transcendentals=rows * hidden,
        ),
        name="feed",
    )(normed, upstream, *pieces)


def rotate_rows(v, cosine, sine):
    half = HD // 2
    low, high = v[:, :half], v[:, half:]
    return jnp.concatenate([low * cosine - high * sine, high * cosine + low * sine], 1)


def feed_plan(hidden):
    tiles = hidden // 128
    threes = next((b for b in range(tiles // 6, 0, -1) if (tiles - 3 * b) % 2 == 0), 0)
    twos = (tiles - 3 * threes) // 2
    if hidden % 128 or not threes or not twos:
        return [(0, hidden, 1)]
    return [(0, 256, twos), (256 * twos, 384, threes)]


def pack_columns(arrays, first, width, chunks):
    cut = [v[:, first : first + width * chunks].reshape(v.shape[0], chunks, width) for v in arrays]
    return jnp.concatenate(cut, 2).reshape(arrays[0].shape[0], -1)


def unpack_columns(v, width, chunks):
    v = v.reshape(v.shape[0], chunks, 3, width)
    return [v[:, :, i].reshape(v.shape[0], -1) for i in range(3)]


def shards(
    tokens,
    cotangent,
    segments,
    positions,
    norm_one,
    qkv_weight,
    qkv_bias,
    out_weight,
    norm_two,
    gate_weight,
    up_weight,
    down_weight,
):
    del segments
    seqs, block, width = tokens.shape
    rows = seqs * block
    per_group = qkv_weight.shape[2]
    q_width = out_weight.shape[1]
    count = lax.axis_size("ctx")
    tp = lax.axis_size("tp")
    half_len = block // tp
    half_start = lax.axis_index("tp") * half_len

    attention_full = jnp.concatenate(gather_plane(jnp.concatenate([qkv_weight[:, 0], out_weight], 1)), 0)
    qkv_full = attention_full[:, :per_group]
    out_full = attention_full[:, per_group:]
    plan = feed_plan(gate_weight.shape[1])
    routes = [(gather_line, scatter_line), (gather_plane, scatter_plane)]
    feed_pieces = [
        gather(pack_columns([gate_weight, up_weight, down_weight], *group))
        for group, (gather, _) in zip(plan, routes)
    ]

    order = order_matrix(width)
    x_low = to_relative(tokens.reshape(rows, width), order)
    upstream_low = to_relative(cotangent.reshape(rows, width), order)
    gains = to_relative(jnp.stack([norm_one, norm_two]), order).astype(f32)
    gain_one, gain_two = gains[0:1], gains[1:2]

    inputs = x_low.astype(f32)
    scale_one = lax.rsqrt(jnp.mean(inputs * inputs, -1, keepdims=True) + epsilon)
    unit_one = inputs * scale_one
    normed = (unit_one * gain_one).astype(bf16)

    projected = mm(qkv_full, normed, contract_first_last) + qkv_bias[0].astype(f32)[:, None]
    frequency = rope_base ** (-(jnp.arange(HD // 2, dtype=f32) * 2.0) / HD)
    angles = positions.reshape(1, rows).astype(f32) * frequency[:, None]
    cosine, sine = jnp.cos(angles), jnp.sin(angles)
    turned = rotate_rows(
        projected[: (GROUP + 1) * HD].reshape(GROUP + 1, HD, rows), cosine, sine
    )
    queries = (turned[:GROUP] * HD ** (-0.5)).astype(bf16).reshape(GROUP * HD, rows)
    kv_t = jnp.concatenate([turned[GROUP], projected[(GROUP + 1) * HD :]], 0).astype(bf16)
    kv_own = kv_t.T.reshape(seqs, block, 2 * HD)
    kv_blocks = [kv_own]
    for s in range(1, count):
        kv_blocks.append(lax.ppermute(kv_own, "ctx", [(i, i + s) for i in range(count - s)]))
    kv = jnp.stack(kv_blocks, 1)
    kv_turned = jnp.swapaxes(kv, 2, 3)
    keys_t, values_t = kv_turned[:, :, :HD], kv_turned[:, :, HD:]
    place = jnp.arange(block, dtype=jnp.int32)
    reach = jnp.max(positions - place[None], 1)
    counts = 1 + jnp.minimum((jnp.maximum(reach, 0) + block - 1) // block, lax.axis_index("ctx"))
    counts = counts.astype(jnp.int32)
    pos = positions.reshape(seqs, 1, block)

    mixed, lse = attend(counts, queries, pos, kv, values_t, block)
    branch = sum_tp(mm(mixed, out_full, contract_first_last))
    middle = inputs + branch
    scale_two = lax.rsqrt(jnp.mean(middle * middle, -1, keepdims=True) + epsilon)
    unit_two = middle * scale_two
    normed_two = (unit_two * gain_two).astype(bf16)

    feed_out, normed_two_part, feed_grads = [], [], []
    for (first, chunk, chunks), pieces, (_, scatter) in zip(plan, feed_pieces, routes):
        out_low, part_low, *grads = feed_group(normed_two, upstream_low, pieces, chunk)
        feed_out.append(out_low)
        normed_two_part.append(part_low)
        feed_grads.append(unpack_columns(scatter(grads), chunk, chunks))
    feed_out = sum(v.astype(f32) for v in feed_out)
    normed_two_part = sum(v.astype(f32) for v in normed_two_part)
    feed_grads = [jnp.concatenate([p[j] for p in feed_grads], 1) for j in range(3)]

    feed_low = feed_out.astype(bf16).reshape(seqs, block, width)

    def own_rows(v, start):
        return lax.dynamic_slice_in_dim(v, start, half_len, 1)

    other_start = (half_len * (tp - 1) - half_start) if tp == 2 else None
    feed_other = swap_tp(own_rows(feed_low, other_start))
    feed_sum = own_rows(feed_low, half_start).astype(f32) + feed_other.astype(f32)
    block_low = (own_rows(middle.reshape(seqs, block, width), half_start) + feed_sum).astype(bf16)
    block_out = to_canonical(block_low.reshape(-1, width), order).reshape(seqs, half_len, width)

    normed_two_grad = sum_tp(normed_two_part)
    gain_two_grad = jnp.sum(normed_two_grad * unit_two, 0, keepdims=True)
    scaled_two = normed_two_grad * gain_two
    middle_grad = upstream_low.astype(f32) + scale_two * (
        scaled_two - unit_two * jnp.mean(scaled_two * unit_two, -1, keepdims=True)
    )
    branch_low = middle_grad.astype(bf16)
    mixed_grad = mm(out_full, branch_low, contract_first_last).astype(bf16)
    out_weight_grad = mm(branch_low, mixed, contract_first_last_rows).astype(bf16)

    query_grads, pack_grads = attend_back(
        counts, queries, pos, kv, keys_t, mixed, lse, mixed_grad, block
    )
    pack_sum = pack_grads[:, 0].astype(f32)
    for s in range(1, count):
        pack_sum = pack_sum + lax.ppermute(
            pack_grads[:, s], "ctx", [(i + s, i) for i in range(count - s)]
        ).astype(f32)
    pack_t = pack_sum.reshape(rows, 2 * HD).T
    grouped = jnp.concatenate([query_grads, pack_t[:HD]], 0).reshape(GROUP + 1, HD, rows)
    turned_back = rotate_rows(grouped, cosine, -sine).reshape((GROUP + 1) * HD, rows)
    projected_grad = jnp.concatenate([turned_back, pack_t[HD:]], 0).astype(bf16)
    bias_grad = jnp.sum(projected_grad.astype(f32), 1)[None]
    qkv_weight_grad = mm(normed, projected_grad, contract_first_last_rows).astype(bf16)
    attention_total = scatter_plane(row_pieces(jnp.concatenate([qkv_weight_grad, out_weight_grad], 1)))

    normed_one_grad = sum_tp(mm(projected_grad, qkv_full, contract_first_last))
    gain_one_grad = jnp.sum(normed_one_grad * unit_one, 0, keepdims=True)
    scaled_one = normed_one_grad * gain_one
    input_grad = middle_grad + scale_one * (
        scaled_one - unit_one * jnp.mean(scaled_one * unit_one, -1, keepdims=True)
    )
    input_grad = to_canonical(input_grad.astype(bf16), order).astype(f32)
    gain_grads = jnp.concatenate([gain_one_grad, gain_two_grad], 0)
    if order is not None:
        gain_grads = lax.dot_general(
            gain_grads, order.astype(f32), contract_last, precision=lax.Precision.HIGHEST
        )
    small = sum_all(jnp.concatenate([gain_grads.reshape(1, -1), bias_grad], 1))
    gain_total = small[:, : 2 * width].reshape(2, width)
    bias_total = small[:, 2 * width :]
    return (
        block_out,
        input_grad.reshape(seqs, block, width),
        gain_total[0],
        attention_total[:, :per_group][:, None, :],
        bias_total,
        attention_total[:, per_group:],
        gain_total[1],
        feed_grads[0],
        feed_grads[1],
        feed_grads[2],
    )


contract_first_last_rows = (((0,), (1,)), ((), ()))


def solution(mesh):
    weight = P(("fsdp", "ctx"), "tp")
    return jax.shard_map(
        shards,
        mesh=mesh,
        in_specs=(
            P("fsdp", "ctx", None),
            P("fsdp", "ctx", None),
            P("fsdp", None),
            P("fsdp", "ctx"),
            P(),
            P(("fsdp", "ctx"), "tp", None),
            P("tp", None),
            weight,
            P(),
            weight,
            weight,
            weight,
        ),
        out_specs=(
            P("fsdp", ("ctx", "tp"), None),
            P("fsdp", "ctx", None),
            P(),
            P(("fsdp", "ctx"), "tp", None),
            P("tp", None),
            weight,
            P(),
            weight,
            weight,
            weight,
        ),
        check_vma=False,
    )
```

```python
import functools

import jax
import jax.numpy as jnp
from jax import lax
from jax.experimental import pallas as pl
from jax.experimental.pallas import tpu as pltpu
from jax.sharding import PartitionSpec as P

HD = 64
GROUP = 7

epsilon = 1e-06
rope_base = 1000000.0
masked_value = -1e30
contract_rows = (((0,), (0,)), ((), ()))
contract_last = (((1,), (1,)), ((), ()))
contract_first_last = (((0,), (1,)), ((), ()))
f32 = jnp.float32
bf16 = jnp.bfloat16


def mm(a, b, dims=(((1,), (0,)), ((), ()))):
    return lax.dot_general(a, b, dims, preferred_element_type=f32)


def after_all(values, *deps):
    return lax.optimization_barrier((*values, *deps))[: len(values)]


def swap_tp(v):
    n = lax.axis_size("tp")
    return lax.ppermute(v, "tp", [(i, (i + 1) % n) for i in range(n)])


def sum_tp(part):
    low = part.astype(bf16)
    return low.astype(f32) + swap_tp(low).astype(f32)


def swap_x(v):
    return lax.ppermute(v, "fsdp", [(i, i ^ 1) for i in range(4)])


def swap_y(v):
    return lax.ppermute(v, "fsdp", [(i, i ^ 2) for i in range(4)])


def exchange(v, axis):
    return lax.all_to_all(v, axis, 0, 0)


def spread(v, axis):
    return exchange(jnp.broadcast_to(v[None], (lax.axis_size(axis),) + v.shape), axis)


def after(v, *deps):
    return lax.optimization_barrier((v, *deps))[0]


def sum_all(v):
    return jnp.sum(spread(v, ("fsdp", "ctx")), 0)


def square_plane():
    return lax.axis_size("fsdp") == 4


def gather_line(w):
    return spread(w, "ctx").reshape(-1, w.shape[1])


def gather_rows(line):
    return spread(line, "fsdp").reshape(-1, line.shape[1])


def gather_pieces(line, far=None):
    if not square_plane():
        return [gather_rows(line)]
    xs, ys = swap_x(line), swap_y(line)
    if far is not None:
        return [line, xs, ys, far]
    half = line.shape[0] // 2
    return [line, xs, ys, swap_y(xs[:half]), swap_x(ys[half:])]


def piece_starts(rows):
    if not square_plane():
        return jnp.zeros((1,), jnp.int32)
    me = lax.axis_index("fsdp")
    far = (me ^ 3) * rows
    return jnp.stack([me * rows, (me ^ 1) * rows, (me ^ 2) * rows, far, far + rows // 2]).astype(jnp.int32)


def swap_xy(v):
    return lax.ppermute(v, "fsdp", [(i, i ^ 3) for i in range(4)])


def add_low(*terms):
    return sum(t.astype(f32) for t in terms).astype(bf16)


def sum_line(v):
    count = lax.axis_size("ctx")
    return jnp.sum(exchange(v.reshape(count, -1, v.shape[1]), "ctx").astype(f32), 0)


def sum_plane(g):
    n = lax.axis_size("fsdp")
    return jnp.sum(exchange(g.reshape(n, -1, g.shape[1]), "fsdp").astype(f32), 0).astype(bf16)


def start_far(pieces):
    return (*pieces[:3], swap_y(pieces[3]), swap_x(pieces[4]))


def finish_far(state, dep):
    own, gx, gy, r1, r2 = after_all(state, dep)
    half = own.shape[0] // 2
    gx = jnp.concatenate([add_low(gx[:half], r1), gx[half:]], 0)
    gy = jnp.concatenate([gy[:half], add_low(gy[half:], r2)], 0)
    return own, gx, gy


def start_near(state):
    own, gx, gy = state
    return own, swap_x(gx), swap_y(gy)


def finish_plane(state, dep):
    return add_low(*after_all(state, dep))


def finish_near(state, dep):
    terms = after_all(state, dep)
    n = lax.axis_size("ctx")
    rows = terms[0].shape[0] // n
    blocks = []
    for i in range(n):
        start = (lax.axis_index("ctx") + i) % n * rows
        blocks.append(add_low(*(lax.dynamic_slice_in_dim(t, start, rows, 0) for t in terms)))
    return blocks


def start_line(blocks):
    n = len(blocks)
    moved = [
        lax.ppermute(blocks[i], "ctx", [(j, (j + i) % n) for j in range(n)]) for i in range(1, n)
    ]
    return [blocks[0]] + moved


def finish_line(blocks, dep):
    return sum(v.astype(f32) for v in after_all(blocks, dep))


def allowed_pairs(pos, offset, keys, block):
    gap = (
        lax.broadcasted_iota(jnp.int32, (keys, block), 1)
        - lax.broadcasted_iota(jnp.int32, (keys, block), 0)
        + offset
    )
    return (gap >= 0) & (gap <= pos)


def attend_kernel(
    seq, count_ref, q_ref, pos_ref, kv_ref, vt_ref, _, o_ref, lse_ref, m_ref, l_ref, acc_ref
):
    block = q_ref.shape[1]
    pos = pos_ref[0]
    m_ref[...] = jnp.full(m_ref.shape, masked_value, f32)
    l_ref[...] = jnp.zeros(l_ref.shape, f32)
    acc_ref[...] = jnp.zeros(acc_ref.shape, f32)

    def step(s, carry):
        keep = allowed_pairs(pos, s * block, block, block)
        keys = kv_ref[0, s, :, :HD]
        values_t = vt_ref[0, s]
        for g in range(GROUP):
            rows = slice(g * HD, (g + 1) * HD)
            scores = jnp.where(keep, mm(keys, q_ref[rows, :]), masked_value)
            old = m_ref[g : g + 1, :]
            top = jnp.maximum(old, jnp.max(scores, 0, keepdims=True))
            weight = jnp.exp(scores - top)
            shrink = jnp.exp(old - top)
            m_ref[g : g + 1, :] = top
            l_ref[g : g + 1, :] = l_ref[g : g + 1, :] * shrink + jnp.sum(weight, 0, keepdims=True)
            acc_ref[rows, :] = acc_ref[rows, :] * shrink + mm(values_t, weight.astype(bf16))
        return carry

    lax.fori_loop(0, count_ref[seq], step, 0)
    for g in range(GROUP):
        rows = slice(g * HD, (g + 1) * HD)
        total = l_ref[g : g + 1, :]
        o_ref[rows, :] = (acc_ref[rows, :] / total).astype(bf16)
        lse_ref[0, g : g + 1, :] = m_ref[g : g + 1, :] + jnp.log(total)
    lse_ref[0, GROUP : GROUP + 1, :] = jnp.zeros((1, block), f32)


def attend_back_kernel(
    count_ref, q_ref, pos_ref, kv_ref, kt_ref, o_ref, lse_ref, do_ref, table_ref,
    dq_ref, dkv_ref, dq_acc
):
    block = q_ref.shape[1]
    last = count_ref.shape[0] - 1
    pos = pos_ref[0]
    dkv_ref[...] = jnp.zeros(dkv_ref.shape, bf16)
    dq_acc[...] = jnp.zeros(dq_acc.shape, f32)

    def step(s, carry):
        keep = allowed_pairs(pos, s * block, block, block)
        keys = kv_ref[0, s, :, :HD]
        values = kv_ref[0, s, :, HD:]
        keys_t = kt_ref[0, s]
        key_grad = jnp.zeros((block, HD), f32)
        value_grad = jnp.zeros((block, HD), f32)
        for g in range(GROUP):
            rows = slice(g * HD, (g + 1) * HD)
            query = q_ref[rows, :]
            grad = do_ref[rows, :]
            centre = jnp.sum(grad.astype(f32) * o_ref[rows, :].astype(f32), 0, keepdims=True)
            scores = mm(keys, query) - lse_ref[0, g : g + 1, :]
            probs = jnp.exp(jnp.where(keep, scores, masked_value))
            prob_grad = mm(values, grad)
            score_grad = (probs * (prob_grad - centre)).astype(bf16)
            value_grad = value_grad + mm(probs.astype(bf16), grad, contract_last)
            key_grad = key_grad + mm(score_grad, query, contract_last)
            dq_acc[rows, :] += mm(keys_t, score_grad)
        dkv_ref[count_ref[last] - s, 0, :, :HD] = key_grad.astype(bf16)
        dkv_ref[count_ref[last] - s, 0, :, HD:] = value_grad.astype(bf16)
        return carry

    lax.fori_loop(0, count_ref[pl.program_id(0)], step, 0)
    cosine, sine = table_ref[: HD // 2, :], table_ref[HD // 2 :, :]
    for g in range(GROUP):
        low = dq_acc[g * HD : g * HD + HD // 2, :] * HD ** (-0.5)
        high = dq_acc[g * HD + HD // 2 : (g + 1) * HD, :] * HD ** (-0.5)
        dq_ref[g * HD : g * HD + HD // 2, :] = (low * cosine + high * sine).astype(bf16)
        dq_ref[g * HD + HD // 2 : (g + 1) * HD, :] = (high * cosine - low * sine).astype(bf16)


def attention_specs(seq, block, count):
    return dict(
        wide=pl.BlockSpec((GROUP * HD, block), lambda i, *_: (0, seq + i)),
        pos=pl.BlockSpec((1, 1, block), lambda i, *_: (seq + i, 0, 0)),
        kv=pl.BlockSpec((1, count, block, 2 * HD), lambda i, *_: (seq + i, 0, 0, 0)),
        half=pl.BlockSpec((1, count, HD, block), lambda i, *_: (seq + i, 0, 0, 0)),
        lse=pl.BlockSpec((1, GROUP + 1, block), lambda i, *_: (i, 0, 0)),
        table=pl.BlockSpec((HD, block), lambda i, *_: (0, seq + i)),
        dkv=pl.BlockSpec((count, 1, block, 2 * HD), lambda i, *_: (0, i, 0, 0)),
        rest=pl.BlockSpec(memory_space=pl.ANY),
    )


VMEM_BYTES = 48 * 1024 * 1024


def attend(seq, counts, queries, pos, kv, values_t, mixed, block):
    count = kv.shape[1]
    spec = attention_specs(seq, block, count)
    work = GROUP * block * block * count
    return pl.pallas_call(
        functools.partial(attend_kernel, seq),
        grid_spec=pltpu.PrefetchScalarGridSpec(
            num_scalar_prefetch=1,
            grid=(1,),
            in_specs=[spec["wide"], spec["pos"], spec["kv"], spec["half"], spec["rest"]],
            out_specs=[spec["wide"], spec["lse"]],
            scratch_shapes=[
                pltpu.VMEM((GROUP + 1, block), f32),
                pltpu.VMEM((GROUP + 1, block), f32),
                pltpu.VMEM((GROUP * HD, block), f32),
            ],
        ),
        out_shape=[
            jax.ShapeDtypeStruct(queries.shape, bf16),
            jax.ShapeDtypeStruct((1, GROUP + 1, block), f32),
        ],
        input_output_aliases={5: 0},
        compiler_params=pltpu.CompilerParams(vmem_limit_bytes=VMEM_BYTES),
        cost_estimate=pl.CostEstimate(
            flops=4 * HD * work * 4, bytes_accessed=2 * 1024 * 1024, transcendentals=work
        ),
        name="attend",
    )(counts, queries, pos, kv, values_t, mixed)


def attend_back(counts, queries, pos, kv, keys_t, mixed, lse, mixed_grad, tables, block):
    seqs, count = kv.shape[:2]
    spec = attention_specs(0, block, count)
    work = seqs * GROUP * block * block * count
    return pl.pallas_call(
        attend_back_kernel,
        grid_spec=pltpu.PrefetchScalarGridSpec(
            num_scalar_prefetch=1,
            grid=(seqs,),
            in_specs=[
                spec["wide"], spec["pos"], spec["kv"], spec["half"],
                spec["wide"], spec["lse"], spec["wide"], spec["table"],
            ],
            out_specs=[spec["wide"], spec["dkv"]],
            scratch_shapes=[pltpu.VMEM((GROUP * HD, block), f32)],
        ),
        out_shape=[
            jax.ShapeDtypeStruct(queries.shape, bf16),
            jax.ShapeDtypeStruct((count, seqs, block, 2 * HD), bf16),
        ],
        compiler_params=pltpu.CompilerParams(vmem_limit_bytes=VMEM_BYTES),
        cost_estimate=pl.CostEstimate(
            flops=10 * HD * work * 4, bytes_accessed=8 * 1024 * 1024, transcendentals=work
        ),
        name="attend_back",
    )(counts, queries, pos, kv, keys_t, mixed, lse, mixed_grad, tables)


def feed_kernel(k, grads, width, tile, start_ref, *refs):
    n_ref, c_ref = refs[:2]
    w_refs = refs[2 : 2 + k]
    out_ref, dn_ref = refs[2 + k : 4 + k]
    g_refs = refs[4 + k : 4 + k + grads]
    gate_up, down, n_t, c_t, hidden_s, pair_s, grad_s, out_acc, dn_acc = refs[4 + k + grads :]
    step = pl.program_id(0)

    @pl.when(step == 0)
    def _():
        n_t[...] = n_ref[...].T
        c_t[...] = c_ref[...].T
        out_acc[...] = jnp.zeros(out_acc.shape, f32)
        dn_acc[...] = jnp.zeros(dn_acc.shape, f32)

    def piece_rows(i, size):
        return pl.ds(pl.multiple_of(start_ref[i], size), size)

    for i, w_ref in enumerate(w_refs):
        rows = piece_rows(i, w_ref.shape[0])
        gate_up[rows, :] = w_ref[:, : 2 * width]
        down[rows, :] = w_ref[:, 2 * width :]

    def token_tile(t, carry):
        rows = pl.ds(pl.multiple_of(t * tile, tile), tile)
        both = mm(n_ref[rows, :], gate_up[...])
        hidden_grad = mm(c_ref[rows, :], down[...])
        gate, up = both[:, :width], both[:, width:]
        sigmoid = jax.nn.sigmoid(gate)
        silu = gate * sigmoid
        hidden = (silu * up).astype(bf16)
        gate_grad = hidden_grad * up * (sigmoid * (1.0 + gate * (1.0 - sigmoid)))
        pair = jnp.concatenate([gate_grad.astype(bf16), (hidden_grad * silu).astype(bf16)], 1)
        hidden_s[rows, :] = hidden
        pair_s[rows, :] = pair
        out_acc[rows, :] += mm(hidden, down[...], contract_last)
        dn_acc[rows, :] += mm(pair, gate_up[...], contract_last)
        return carry

    lax.fori_loop(0, n_ref.shape[0] // tile, token_tile, 0)
    grad_s[:, : 2 * width] = mm(n_t[...], pair_s[...]).astype(bf16)
    grad_s[:, 2 * width :] = mm(c_t[...], hidden_s[...]).astype(bf16)
    for i, g_ref in enumerate(g_refs):
        g_ref[...] = grad_s[piece_rows(i, g_ref.shape[0]), :]

    @pl.when(step == pl.num_programs(0) - 1)
    def _():
        out_ref[...] = out_acc[...].astype(bf16)
        dn_ref[...] = dn_acc[...].astype(bf16)


def feed_group(normed, upstream, pieces, width, chunks):
    rows, model = normed.shape
    tile = min(rows, 256)
    whole = pl.BlockSpec((rows, model), lambda j, *_: (0, 0))
    blocks = [pl.BlockSpec((p.shape[0], 3 * width), lambda j, *_: (0, j)) for p in pieces]
    hidden = chunks * width
    sizes = [p.shape[0] for p in pieces]
    if square_plane():
        sizes = sizes[:3] + [sizes[0] // 2] * 2
    grads = [pl.BlockSpec((r, 3 * width), lambda j, *_: (0, j)) for r in sizes]
    return pl.pallas_call(
        functools.partial(feed_kernel, len(pieces), len(sizes), width, tile),
        grid_spec=pltpu.PrefetchScalarGridSpec(
            num_scalar_prefetch=1,
            grid=(chunks,),
            in_specs=[whole, whole] + blocks,
            out_specs=[whole, whole] + grads,
            scratch_shapes=[
                pltpu.VMEM((model, 2 * width), bf16),
                pltpu.VMEM((model, width), bf16),
                pltpu.VMEM((model, rows), bf16),
                pltpu.VMEM((model, rows), bf16),
                pltpu.VMEM((rows, width), bf16),
                pltpu.VMEM((rows, 2 * width), bf16),
                pltpu.VMEM((model, 3 * width), bf16),
                pltpu.VMEM((rows, model), f32),
                pltpu.VMEM((rows, model), f32),
            ],
        ),
        out_shape=[jax.ShapeDtypeStruct((rows, model), bf16)] * 2
        + [jax.ShapeDtypeStruct((r, 3 * width * chunks), bf16) for r in sizes],
        compiler_params=pltpu.CompilerParams(vmem_limit_bytes=VMEM_BYTES),
        cost_estimate=pl.CostEstimate(
            flops=18 * rows * model * hidden,
            bytes_accessed=12 * model * hidden + 8 * rows * model,
            transcendentals=rows * hidden,
        ),
        name="feed",
    )(piece_starts(pieces[0].shape[0]), normed, upstream, *pieces)


def rotate_rows(v, cosine, sine):
    half = HD // 2
    low, high = v[:, :half], v[:, half:]
    return jnp.concatenate([low * cosine - high * sine, high * cosine + low * sine], 1)


def feed_plan(hidden):
    tiles = hidden // 128
    threes = next((b for b in range(tiles // 6, 0, -1) if (tiles - 3 * b) % 2 == 0), 0)
    if hidden % 128 or not threes:
        return [(0, hidden, 1)]
    return [(0, 384, threes), (384 * threes, 256, (tiles - 3 * threes) // 2)]


def pack_columns(arrays, first, width, chunks):
    cut = [v[:, first : first + width * chunks].reshape(v.shape[0], chunks, width) for v in arrays]
    return jnp.concatenate(cut, 2).reshape(arrays[0].shape[0], -1)


def unpack_columns(v, width, chunks):
    v = v.reshape(v.shape[0], chunks, 3, width)
    return [v[:, :, i].reshape(v.shape[0], -1) for i in range(3)]


def shards(
    tokens,
    cotangent,
    segments,
    positions,
    norm_one,
    qkv_weight,
    qkv_bias,
    out_weight,
    norm_two,
    gate_weight,
    up_weight,
    down_weight,
):
    del segments
    seqs, block, width = tokens.shape
    rows = seqs * block
    count = lax.axis_size("ctx")
    tp = lax.axis_size("tp")
    half_len = block // tp
    half_start = lax.axis_index("tp") * half_len

    query_cols = GROUP * HD
    every = ("fsdp", "ctx")
    kv_full = spread(qkv_weight[:, 0, query_cols:], every).reshape(width, -1)
    query_full = gather_rows(gather_line(after(qkv_weight[:, 0, :query_cols], kv_full)))

    inputs = tokens.reshape(rows, width).astype(f32)
    upstream_low = cotangent.reshape(rows, width)
    gain_one, gain_two = norm_one.astype(f32)[None], norm_two.astype(f32)[None]
    scale_one = lax.rsqrt(jnp.mean(inputs * inputs, -1, keepdims=True) + epsilon)
    unit_one = inputs * scale_one
    normed = (unit_one * gain_one).astype(bf16)

    bias = qkv_bias[0].astype(f32)[:, None]
    frequency = rope_base ** (-(jnp.arange(HD // 2, dtype=f32) * 2.0) / HD)
    angles = positions.reshape(1, rows).astype(f32) * frequency[:, None]
    cosine, sine = jnp.cos(angles), jnp.sin(angles)
    tables = jnp.concatenate([cosine, sine], 0)
    kv_projected = mm(kv_full, normed, contract_first_last) + bias[query_cols:]
    turned_key = rotate_rows(kv_projected[None, :HD], cosine, sine)[0]
    kv_t = jnp.concatenate([turned_key, kv_projected[HD:]], 0).astype(bf16)
    kv_own = kv_t.T.reshape(seqs, block, 2 * HD)
    kv_blocks = [kv_own]
    for s in range(1, count):
        kv_blocks.append(lax.ppermute(kv_own, "ctx", [(i, i + s) for i in range(count - s)]))
    plan = feed_plan(gate_weight.shape[1])
    packs = [pack_columns([gate_weight, up_weight, down_weight], *group) for group in plan]
    packs[0] = jnp.concatenate([packs[0], out_weight], 1)
    lines = [gather_line(after(packs[0], query_full, *kv_blocks[1:]))]
    far_packs = [swap_xy(after(own, kv_full)) for own in packs[1:]] if square_plane() else []
    kv = jnp.stack(after_all(kv_blocks, *far_packs), 1)
    kv_turned = jnp.swapaxes(kv, 2, 3)
    keys_t, values_t = kv_turned[:, :, :HD], kv_turned[:, :, HD:]
    projected = mm(query_full, normed, contract_first_last) + bias[:query_cols]
    turned = rotate_rows(projected.reshape(GROUP, HD, rows), cosine, sine)
    queries = (turned * HD ** (-0.5)).astype(bf16).reshape(query_cols, rows)
    place = jnp.arange(block, dtype=jnp.int32)
    reach = jnp.max(positions - place[None], 1)
    counts = 1 + jnp.minimum((jnp.maximum(reach, 0) + block - 1) // block, lax.axis_index("ctx"))
    counts = jnp.concatenate([counts, lax.axis_index("ctx")[None]]).astype(jnp.int32)
    pos = positions.reshape(seqs, 1, block)

    mixed, log_totals = jnp.zeros(queries.shape, bf16), []
    ready = queries
    for s in range(seqs):
        mixed, lse = attend(s, counts, ready, pos, kv, values_t, mixed, block)
        log_totals.append(lse)
    lines[0] = after(lines[0], mixed)
    for own in packs[1:]:
        lines.append(gather_line(after(own, lines[-1])))
    far_lines = [gather_line(after(own, lines[-1])) for own in far_packs]
    feed_pieces = [gather_pieces(lines[0])]
    for i, line in enumerate(lines[1:]):
        feed_pieces.append(gather_pieces(line, far_lines[i] if far_lines else None))
    out_full = jnp.zeros((width, query_cols), bf16)
    for start, piece in zip(piece_starts(feed_pieces[0][0].shape[0]), feed_pieces[0]):
        out_full = lax.dynamic_update_slice_in_dim(out_full, piece[:, -query_cols:], start, 0)
    branch = sum_tp(mm(mixed, out_full, contract_first_last))
    middle = inputs + branch
    scale_two = lax.rsqrt(jnp.mean(middle * middle, -1, keepdims=True) + epsilon)
    unit_two = middle * scale_two
    normed_two = (unit_two * gain_two).astype(bf16)

    feed_out, normed_two_part, far, near, blocks = [], [], [], [], []
    turn = normed_two
    staged = square_plane() and len(plan) == 2
    for i, ((first, chunk, chunks), pieces) in enumerate(zip(plan, feed_pieces)):
        if i + 1 < len(plan):
            turn = after(turn, lines[i + 1])
        out_low, part_low, *parts = feed_group(turn, upstream_low, pieces, chunk, chunks)
        feed_out.append(out_low)
        normed_two_part.append(part_low)
        turn = after(normed_two, part_low)
        if not staged:
            far.append(parts)
            continue
        if far:
            near.append(start_near(finish_far(far[-1], part_low)))
        far.append(start_far(parts))
    feed_out = sum(v.astype(f32) for v in feed_out)
    normed_two_part = sum(v.astype(f32) for v in normed_two_part)

    feed_low = feed_out.astype(bf16).reshape(seqs, block, width)

    def own_rows(v, start):
        return lax.dynamic_slice_in_dim(v, start, half_len, 1)

    other_start = (half_len * (tp - 1) - half_start) if tp == 2 else None
    feed_other = swap_tp(own_rows(feed_low, other_start))
    feed_sum = own_rows(feed_low, half_start).astype(f32) + feed_other.astype(f32)
    block_low = (own_rows(middle.reshape(seqs, block, width), half_start) + feed_sum).astype(bf16)
    block_out = block_low

    normed_two_grad = sum_tp(normed_two_part)
    gain_two_grad = jnp.sum(normed_two_grad * unit_two, 0, keepdims=True)
    scaled_two = normed_two_grad * gain_two
    middle_grad = upstream_low.astype(f32) + scale_two * (
        scaled_two - unit_two * jnp.mean(scaled_two * unit_two, -1, keepdims=True)
    )
    branch_low = middle_grad.astype(bf16)
    mixed_grad = mm(out_full, branch_low, contract_first_last).astype(bf16)
    out_weight_grad = mm(branch_low, mixed, contract_first_last_rows).astype(bf16)

    feed_totals, grad_in = [], mixed_grad
    if staged:
        second_far = finish_far(far[1], branch_low)
        grad_in = after(grad_in, *second_far)
        near.append(start_near(second_far))
    query_grads, pack_grads = attend_back(
        counts, queries, pos, kv, keys_t, mixed, jnp.concatenate(log_totals, 0), grad_in, tables,
        block,
    )
    if staged:
        blocks = finish_near(near[0], pack_grads)
        query_grads, pack_grads = after_all((query_grads, pack_grads), *blocks)
        line = start_line(blocks)
    pack_sum = jnp.sum(exchange(pack_grads, "ctx").astype(f32), 0)
    normed_one_part = mm(query_grads, query_full, contract_first_last)
    query_weight_grad = mm(normed, query_grads, contract_first_last_rows).astype(bf16)
    pack_t = pack_sum.reshape(rows, 2 * HD).T
    turned_back = rotate_rows(pack_t[None, :HD], cosine, -sine)[0]
    kv_grads = jnp.concatenate([turned_back, pack_t[HD:]], 0).astype(bf16)
    kv_weight_grad = mm(normed, kv_grads, contract_first_last_rows).astype(bf16)
    weight_grads = jnp.concatenate([query_weight_grad, kv_weight_grad, out_weight_grad], 1)
    attention_plane = sum_plane(weight_grads)
    attention_total = sum_line(attention_plane)
    kv_grads = after(kv_grads, weight_grads)
    if staged:
        feed_totals.append(finish_line(line, attention_plane))
        feed_totals.append(
            sum(v.astype(f32) for v in start_line(finish_near(near[1], attention_plane)))
        )
    else:
        for g in far:
            if square_plane():
                g = finish_near(start_near(finish_far(start_far(g), normed)), normed)
                feed_totals.append(sum(v.astype(f32) for v in start_line(g)))
            else:
                feed_totals.append(sum_line(sum_plane(g[0])))
    feed_grads = [
        unpack_columns(v, chunk, chunks) for v, (_, chunk, chunks) in zip(feed_totals, plan)
    ]
    feed_grads = [jnp.concatenate([p[j] for p in feed_grads], 1) for j in range(3)]
    bias_grad = jnp.concatenate(
        [jnp.sum(query_grads.astype(f32), 1), jnp.sum(kv_grads.astype(f32), 1)]
    )[None]

    normed_one_grad = sum_tp(normed_one_part + mm(kv_grads, kv_full, contract_first_last))
    gain_one_grad = jnp.sum(normed_one_grad * unit_one, 0, keepdims=True)
    scaled_one = normed_one_grad * gain_one
    input_grad = middle_grad + scale_one * (
        scaled_one - unit_one * jnp.mean(scaled_one * unit_one, -1, keepdims=True)
    )
    input_grad = input_grad.astype(bf16).astype(f32)
    gain_grads = jnp.concatenate([gain_one_grad, gain_two_grad], 0)
    small = sum_all(jnp.concatenate([gain_grads.reshape(1, -1), bias_grad], 1))
    gain_total = small[:, : 2 * width].reshape(2, width)
    bias_total = small[:, 2 * width :]
    return (
        block_out,
        input_grad.reshape(seqs, block, width),
        gain_total[0],
        attention_total[:, None, : query_cols + 2 * HD],
        bias_total,
        attention_total[:, query_cols + 2 * HD :],
        gain_total[1],
        feed_grads[0],
        feed_grads[1],
        feed_grads[2],
    )


contract_first_last_rows = (((0,), (1,)), ((), ()))


def solution(mesh):
    weight = P(("fsdp", "ctx"), "tp")
    return jax.shard_map(
        shards,
        mesh=mesh,
        in_specs=(
            P("fsdp", "ctx", None),
            P("fsdp", "ctx", None),
            P("fsdp", None),
            P("fsdp", "ctx"),
            P(),
            P(("fsdp", "ctx"), "tp", None),
            P("tp", None),
            weight,
            P(),
            weight,
            weight,
            weight,
        ),
        out_specs=(
            P("fsdp", ("ctx", "tp"), None),
            P("fsdp", "ctx", None),
            P(),
            P(("fsdp", "ctx"), "tp", None),
            P("tp", None),
            weight,
            P(),
            weight,
            weight,
            weight,
        ),
        check_vma=False,
    )
```

```python
import functools

import jax
import jax.numpy as jnp
from jax import lax
from jax.experimental import pallas as pl
from jax.experimental.pallas import tpu as pltpu
from jax.sharding import PartitionSpec as P

HD = 64
GROUP = 7

epsilon = 1e-06
rope_base = 1000000.0
masked_value = -1e30
contract_rows = (((0,), (0,)), ((), ()))
contract_last = (((1,), (1,)), ((), ()))
contract_first_last = (((0,), (1,)), ((), ()))
f32 = jnp.float32
bf16 = jnp.bfloat16


def mm(a, b, dims=(((1,), (0,)), ((), ()))):
    return lax.dot_general(a, b, dims, preferred_element_type=f32)


def swap_tp(v):
    n = lax.axis_size("tp")
    return lax.ppermute(v, "tp", [(i, (i + 1) % n) for i in range(n)])


def sum_tp(part):
    low = part.astype(bf16)
    return low.astype(f32) + swap_tp(low).astype(f32)


def swap_x(v):
    return lax.ppermute(v, "fsdp", [(i, i ^ 1) for i in range(4)])


def swap_y(v):
    return lax.ppermute(v, "fsdp", [(i, i ^ 2) for i in range(4)])


def ring_up(v):
    n = lax.axis_size("ctx")
    return lax.ppermute(v, "ctx", [(i, (i + 1) % n) for i in range(n)])


def ring_down(v):
    n = lax.axis_size("ctx")
    return lax.ppermute(v, "ctx", [((i + 1) % n, i) for i in range(n)])


def swap_xy(v):
    return lax.ppermute(v, "fsdp", [(i, i ^ 3) for i in range(4)])


def sum_all(v):
    axes = ("fsdp", "ctx")
    count = lax.axis_size("fsdp") * lax.axis_size("ctx")
    return jnp.sum(lax.all_to_all(jnp.broadcast_to(v[None], (count,) + v.shape), axes, 0, 0), 0)


def relative_order():
    return lax.axis_size("fsdp") == 4 and lax.axis_size("ctx") % 2 == 0


def ring_pieces(w):
    pieces = [w]
    for _ in range(lax.axis_size("ctx") - 1):
        pieces.append(ring_up(pieces[-1]))
    return pieces


def gather_plane(w):
    if not relative_order():
        return [lax.all_gather(w, ("fsdp", "ctx"), axis=0, tiled=True)]
    own = jnp.concatenate(ring_pieces(w), 0)
    half = own.shape[0] // 2
    xs, ys = swap_x(own), swap_y(own)
    return [own, xs, ys, swap_y(xs[:half]), swap_x(ys[half:])]


def gather_line(w):
    if not relative_order():
        return [lax.all_gather(w, ("fsdp", "ctx"), axis=0, tiled=True)]
    cols = w.shape[1]
    pieces = ring_pieces(jnp.concatenate([w, swap_xy(w)], 1))
    own = jnp.concatenate([p[:, :cols] for p in pieces], 0)
    far = jnp.concatenate([p[:, cols:] for p in pieces], 0)
    return [own, swap_x(own), swap_y(own), far]


def add_low(*terms):
    return sum(t.astype(f32) for t in terms).astype(bf16)


def ring_sum(v, last=f32):
    total = v[-1]
    for s in range(v.shape[0] - 2, 0, -1):
        total = add_low(ring_down(total), v[s])
    return ring_down(total).astype(f32) + v[0].astype(f32)


def direct_sum(v):
    n = v.shape[0]
    total = v[0].astype(f32)
    for s in range(1, n):
        total = total + lax.ppermute(v[s], "ctx", [(i, (i - s) % n) for i in range(n)]).astype(f32)
    return total


def scatter_plane(pieces, line_sum=ring_sum):
    if not relative_order():
        return lax.psum_scatter(
            pieces[0], ("fsdp", "ctx"), scatter_dimension=0, tiled=True
        ).astype(f32)
    count = lax.axis_size("ctx")
    own, gx, gy, g1, g2 = pieces
    half = own.shape[0] // 2
    r1, r2 = swap_y(g1), swap_x(g2)
    gx = jnp.concatenate([add_low(gx[:half], r1), gx[half:]], 0)
    gy = jnp.concatenate([gy[:half], add_low(gy[half:], r2)], 0)
    plane = add_low(own, swap_x(gx), swap_y(gy))
    return line_sum(plane.reshape(count, -1, own.shape[1]))


def scatter_line(pieces):
    if not relative_order():
        return lax.psum_scatter(
            pieces[0], ("fsdp", "ctx"), scatter_dimension=0, tiled=True
        ).astype(f32)
    count = lax.axis_size("ctx")
    own, gx, gy, far = pieces
    cols = own.shape[1]
    plane = add_low(own, swap_x(gx), swap_y(gy))
    both = jnp.concatenate([plane, far], 1).reshape(count, -1, 2 * cols)
    total = ring_sum(both)
    return total[:, :cols] + swap_xy(total[:, cols:].astype(bf16)).astype(f32)


def row_pieces(g):
    if not relative_order():
        return [g]
    part = g.shape[0] // 8
    ends = [0, 2 * part, 4 * part, 6 * part, 7 * part, 8 * part]
    return [g[a:b] for a, b in zip(ends[:-1], ends[1:])]


def order_matrix(model_width):
    if not relative_order():
        return None
    count = lax.axis_size("ctx")
    rows = model_width // (4 * count)
    place = jnp.arange(model_width, dtype=jnp.int32)
    block = place // rows
    fsdp = lax.axis_index("fsdp") ^ (block // count)
    ctx = (lax.axis_index("ctx") - block % count + count) % count
    source = (fsdp * count + ctx) * rows + place % rows
    return (jnp.arange(model_width, dtype=jnp.int32)[:, None] == source[None, :]).astype(bf16)


def to_relative(v, order):
    return v if order is None else mm(v, order).astype(v.dtype)


def to_canonical(v, order):
    return v if order is None else mm(v, order, contract_last).astype(v.dtype)


def allowed_pairs(pos, offset, keys, block):
    gap = (
        lax.broadcasted_iota(jnp.int32, (keys, block), 1)
        - lax.broadcasted_iota(jnp.int32, (keys, block), 0)
        + offset
    )
    return (gap >= 0) & (gap <= pos)


def attend_kernel(count_ref, q_ref, pos_ref, kv_ref, vt_ref, o_ref, lse_ref, m_ref, l_ref, acc_ref):
    block = q_ref.shape[1]
    pos = pos_ref[0]
    m_ref[...] = jnp.full(m_ref.shape, masked_value, f32)
    l_ref[...] = jnp.zeros(l_ref.shape, f32)
    acc_ref[...] = jnp.zeros(acc_ref.shape, f32)

    def step(s, carry):
        keep = allowed_pairs(pos, s * block, block, block)
        keys = kv_ref[0, s, :, :HD]
        values_t = vt_ref[0, s]
        for g in range(GROUP):
            rows = slice(g * HD, (g + 1) * HD)
            scores = jnp.where(keep, mm(keys, q_ref[rows, :]), masked_value)
            old = m_ref[g : g + 1, :]
            top = jnp.maximum(old, jnp.max(scores, 0, keepdims=True))
            weight = jnp.exp(scores - top)
            shrink = jnp.exp(old - top)
            m_ref[g : g + 1, :] = top
            l_ref[g : g + 1, :] = l_ref[g : g + 1, :] * shrink + jnp.sum(weight, 0, keepdims=True)
            acc_ref[rows, :] = acc_ref[rows, :] * shrink + mm(values_t, weight.astype(bf16))
        return carry

    lax.fori_loop(0, count_ref[pl.program_id(0)], step, 0)
    for g in range(GROUP):
        rows = slice(g * HD, (g + 1) * HD)
        total = l_ref[g : g + 1, :]
        o_ref[rows, :] = (acc_ref[rows, :] / total).astype(bf16)
        lse_ref[0, g : g + 1, :] = m_ref[g : g + 1, :] + jnp.log(total)
    lse_ref[0, GROUP : GROUP + 1, :] = jnp.zeros((1, block), f32)


def attend_back_kernel(
    count_ref, q_ref, pos_ref, kv_ref, kt_ref, o_ref, lse_ref, do_ref, dq_ref, dkv_ref, dq_acc
):
    block = q_ref.shape[1]
    pos = pos_ref[0]
    dkv_ref[...] = jnp.zeros(dkv_ref.shape, bf16)
    dq_acc[...] = jnp.zeros(dq_acc.shape, f32)

    def step(s, carry):
        keep = allowed_pairs(pos, s * block, block, block)
        keys = kv_ref[0, s, :, :HD]
        values = kv_ref[0, s, :, HD:]
        keys_t = kt_ref[0, s]
        key_grad = jnp.zeros((block, HD), f32)
        value_grad = jnp.zeros((block, HD), f32)
        for g in range(GROUP):
            rows = slice(g * HD, (g + 1) * HD)
            query = q_ref[rows, :]
            grad = do_ref[rows, :]
            centre = jnp.sum(grad.astype(f32) * o_ref[rows, :].astype(f32), 0, keepdims=True)
            scores = mm(keys, query) - lse_ref[0, g : g + 1, :]
            probs = jnp.exp(jnp.where(keep, scores, masked_value))
            prob_grad = mm(values, grad)
            score_grad = (probs * (prob_grad - centre)).astype(bf16)
            value_grad = value_grad + mm(probs.astype(bf16), grad, contract_last)
            key_grad = key_grad + mm(score_grad, query, contract_last)
            dq_acc[rows, :] += mm(keys_t, score_grad)
        dkv_ref[0, s, :, :HD] = key_grad.astype(bf16)
        dkv_ref[0, s, :, HD:] = value_grad.astype(bf16)
        return carry

    lax.fori_loop(0, count_ref[pl.program_id(0)], step, 0)
    dq_ref[...] = dq_acc[...] * HD ** (-0.5)


def attention_specs(block, count):
    return dict(
        wide=pl.BlockSpec((GROUP * HD, block), lambda i, *_: (0, i)),
        pos=pl.BlockSpec((1, 1, block), lambda i, *_: (i, 0, 0)),
        kv=pl.BlockSpec((1, count, block, 2 * HD), lambda i, *_: (i, 0, 0, 0)),
        half=pl.BlockSpec((1, count, HD, block), lambda i, *_: (i, 0, 0, 0)),
        lse=pl.BlockSpec((1, GROUP + 1, block), lambda i, *_: (i, 0, 0)),
    )


VMEM_BYTES = 48 * 1024 * 1024


def attend(counts, queries, pos, kv, values_t, block):
    seqs, count = kv.shape[:2]
    spec = attention_specs(block, count)
    work = seqs * GROUP * block * block * count
    return pl.pallas_call(
        attend_kernel,
        grid_spec=pltpu.PrefetchScalarGridSpec(
            num_scalar_prefetch=1,
            grid=(seqs,),
            in_specs=[spec["wide"], spec["pos"], spec["kv"], spec["half"]],
            out_specs=[spec["wide"], spec["lse"]],
            scratch_shapes=[
                pltpu.VMEM((GROUP + 1, block), f32),
                pltpu.VMEM((GROUP + 1, block), f32),
                pltpu.VMEM((GROUP * HD, block), f32),
            ],
        ),
        out_shape=[
            jax.ShapeDtypeStruct((GROUP * HD, seqs * block), bf16),
            jax.ShapeDtypeStruct((seqs, GROUP + 1, block), f32),
        ],
        compiler_params=pltpu.CompilerParams(vmem_limit_bytes=VMEM_BYTES),
        cost_estimate=pl.CostEstimate(
            flops=4 * HD * work * 4, bytes_accessed=4 * 1024 * 1024, transcendentals=work
        ),
        name="attend",
    )(counts, queries, pos, kv, values_t)


def attend_back(counts, queries, pos, kv, keys_t, mixed, lse, mixed_grad, block):
    seqs, count = kv.shape[:2]
    spec = attention_specs(block, count)
    work = seqs * GROUP * block * block * count
    return pl.pallas_call(
        attend_back_kernel,
        grid_spec=pltpu.PrefetchScalarGridSpec(
            num_scalar_prefetch=1,
            grid=(seqs,),
            in_specs=[
                spec["wide"], spec["pos"], spec["kv"], spec["half"],
                spec["wide"], spec["lse"], spec["wide"],
            ],
            out_specs=[spec["wide"], spec["kv"]],
            scratch_shapes=[pltpu.VMEM((GROUP * HD, block), f32)],
        ),
        out_shape=[
            jax.ShapeDtypeStruct((GROUP * HD, seqs * block), f32),
            jax.ShapeDtypeStruct((seqs, count, block, 2 * HD), bf16),
        ],
        compiler_params=pltpu.CompilerParams(vmem_limit_bytes=VMEM_BYTES),
        cost_estimate=pl.CostEstimate(
            flops=10 * HD * work * 4, bytes_accessed=8 * 1024 * 1024, transcendentals=work
        ),
        name="attend_back",
    )(counts, queries, pos, kv, keys_t, mixed, lse, mixed_grad)


def feed_kernel(starts, width, tile, *refs):
    k = len(starts)
    n_ref, c_ref = refs[:2]
    w_refs = refs[2 : 2 + k]
    out_ref, dn_ref = refs[2 + k : 4 + k]
    g_refs = refs[4 + k : 4 + 2 * k]
    gate_up, down, n_t, c_t, hidden_s, pair_s, out_acc, dn_acc = refs[4 + 2 * k :]
    step = pl.program_id(0)

    @pl.when(step == 0)
    def _():
        n_t[...] = n_ref[...].T
        c_t[...] = c_ref[...].T
        out_acc[...] = jnp.zeros(out_acc.shape, f32)
        dn_acc[...] = jnp.zeros(dn_acc.shape, f32)

    for start, w_ref in zip(starts, w_refs):
        rows = slice(start, start + w_ref.shape[0])
        gate_up[rows, :] = w_ref[:, : 2 * width]
        down[rows, :] = w_ref[:, 2 * width :]

    def token_tile(t, carry):
        rows = pl.ds(pl.multiple_of(t * tile, tile), tile)
        both = mm(n_ref[rows, :], gate_up[...])
        hidden_grad = mm(c_ref[rows, :], down[...])
        gate, up = both[:, :width], both[:, width:]
        sigmoid = jax.nn.sigmoid(gate)
        silu = gate * sigmoid
        hidden = (silu * up).astype(bf16)
        gate_grad = hidden_grad * up * (sigmoid * (1.0 + gate * (1.0 - sigmoid)))
        pair = jnp.concatenate([gate_grad.astype(bf16), (hidden_grad * silu).astype(bf16)], 1)
        hidden_s[rows, :] = hidden
        pair_s[rows, :] = pair
        out_acc[rows, :] += mm(hidden, down[...], contract_last)
        dn_acc[rows, :] += mm(pair, gate_up[...], contract_last)
        return carry

    lax.fori_loop(0, n_ref.shape[0] // tile, token_tile, 0)
    pair_grad = mm(n_t[...], pair_s[...]).astype(bf16)
    down_grad = mm(c_t[...], hidden_s[...]).astype(bf16)
    for start, g_ref in zip(starts, g_refs):
        rows = slice(start, start + g_ref.shape[0])
        g_ref[:, : 2 * width] = pair_grad[rows]
        g_ref[:, 2 * width :] = down_grad[rows]

    @pl.when(step == pl.num_programs(0) - 1)
    def _():
        out_ref[...] = out_acc[...].astype(bf16)
        dn_ref[...] = dn_acc[...].astype(bf16)


def feed_group(normed, upstream, pieces, width):
    rows, model = normed.shape
    chunks = pieces[0].shape[1] // (3 * width)
    starts, start = [], 0
    for p in pieces:
        starts.append(start)
        start += p.shape[0]
    tile = min(rows, 256)
    whole = pl.BlockSpec((rows, model), lambda j: (0, 0))
    blocks = [pl.BlockSpec((p.shape[0], 3 * width), lambda j: (0, j)) for p in pieces]
    hidden = chunks * width
    return pl.pallas_call(
        functools.partial(feed_kernel, starts, width, tile),
        grid=(chunks,),
        in_specs=[whole, whole] + blocks,
        out_specs=[whole, whole] + blocks,
        out_shape=[jax.ShapeDtypeStruct((rows, model), bf16)] * 2
        + [jax.ShapeDtypeStruct(p.shape, bf16) for p in pieces],
        scratch_shapes=[
            pltpu.VMEM((model, 2 * width), bf16),
            pltpu.VMEM((model, width), bf16),
            pltpu.VMEM((model, rows), bf16),
            pltpu.VMEM((model, rows), bf16),
            pltpu.VMEM((rows, width), bf16),
            pltpu.VMEM((rows, 2 * width), bf16),
            pltpu.VMEM((rows, model), f32),
            pltpu.VMEM((rows, model), f32),
        ],
        compiler_params=pltpu.CompilerParams(vmem_limit_bytes=VMEM_BYTES),
        cost_estimate=pl.CostEstimate(
            flops=18 * rows * model * hidden,
            bytes_accessed=12 * model * hidden + 8 * rows * model,
            transcendentals=rows * hidden,
        ),
        name="feed",
    )(normed, upstream, *pieces)


def rotate_rows(v, cosine, sine):
    half = HD // 2
    low, high = v[:, :half], v[:, half:]
    return jnp.concatenate([low * cosine - high * sine, high * cosine + low * sine], 1)


def feed_plan(hidden):
    tiles = hidden // 128
    threes = next((b for b in range(tiles // 6, 0, -1) if (tiles - 3 * b) % 2 == 0), 0)
    twos = (tiles - 3 * threes) // 2
    if hidden % 128 or not threes or not twos:
        return [(0, hidden, 1)]
    return [(0, 256, twos), (256 * twos, 384, threes)]


def pack_columns(arrays, first, width, chunks):
    cut = [v[:, first : first + width * chunks].reshape(v.shape[0], chunks, width) for v in arrays]
    return jnp.concatenate(cut, 2).reshape(arrays[0].shape[0], -1)


def unpack_columns(v, width, chunks):
    v = v.reshape(v.shape[0], chunks, 3, width)
    return [v[:, :, i].reshape(v.shape[0], -1) for i in range(3)]


def shards(
    tokens,
    cotangent,
    segments,
    positions,
    norm_one,
    qkv_weight,
    qkv_bias,
    out_weight,
    norm_two,
    gate_weight,
    up_weight,
    down_weight,
):
    del segments
    seqs, block, width = tokens.shape
    rows = seqs * block
    per_group = qkv_weight.shape[2]
    q_width = out_weight.shape[1]
    count = lax.axis_size("ctx")
    tp = lax.axis_size("tp")
    half_len = block // tp
    half_start = lax.axis_index("tp") * half_len

    attention_full = jnp.concatenate(gather_plane(jnp.concatenate([qkv_weight[:, 0], out_weight], 1)), 0)
    qkv_full = attention_full[:, :per_group]
    out_full = attention_full[:, per_group:]
    plan = feed_plan(gate_weight.shape[1])
    routes = [(gather_line, scatter_line), (gather_plane, scatter_plane)]
    feed_pieces = [
        gather(pack_columns([gate_weight, up_weight, down_weight], *group))
        for group, (gather, _) in zip(plan, routes)
    ]

    order = order_matrix(width)
    x_low = to_relative(tokens.reshape(rows, width), order)
    upstream_low = to_relative(cotangent.reshape(rows, width), order)
    gains = to_relative(jnp.stack([norm_one, norm_two]), order).astype(f32)
    gain_one, gain_two = gains[0:1], gains[1:2]

    inputs = x_low.astype(f32)
    scale_one = lax.rsqrt(jnp.mean(inputs * inputs, -1, keepdims=True) + epsilon)
    unit_one = inputs * scale_one
    normed = (unit_one * gain_one).astype(bf16)

    projected = mm(qkv_full, normed, contract_first_last) + qkv_bias[0].astype(f32)[:, None]
    frequency = rope_base ** (-(jnp.arange(HD // 2, dtype=f32) * 2.0) / HD)
    angles = positions.reshape(1, rows).astype(f32) * frequency[:, None]
    cosine, sine = jnp.cos(angles), jnp.sin(angles)
    turned = rotate_rows(
        projected[: (GROUP + 1) * HD].reshape(GROUP + 1, HD, rows), cosine, sine
    )
    queries = (turned[:GROUP] * HD ** (-0.5)).astype(bf16).reshape(GROUP * HD, rows)
    kv_t = jnp.concatenate([turned[GROUP], projected[(GROUP + 1) * HD :]], 0).astype(bf16)
    kv_own = kv_t.T.reshape(seqs, block, 2 * HD)
    kv_blocks = [kv_own]
    for s in range(1, count):
        kv_blocks.append(lax.ppermute(kv_own, "ctx", [(i, i + s) for i in range(count - s)]))
    kv = jnp.stack(kv_blocks, 1)
    kv_turned = jnp.swapaxes(kv, 2, 3)
    keys_t, values_t = kv_turned[:, :, :HD], kv_turned[:, :, HD:]
    place = jnp.arange(block, dtype=jnp.int32)
    reach = jnp.max(positions - place[None], 1)
    counts = 1 + jnp.minimum((jnp.maximum(reach, 0) + block - 1) // block, lax.axis_index("ctx"))
    counts = counts.astype(jnp.int32)
    pos = positions.reshape(seqs, 1, block)

    mixed, lse = attend(counts, queries, pos, kv, values_t, block)
    branch = sum_tp(mm(mixed, out_full, contract_first_last))
    middle = inputs + branch
    scale_two = lax.rsqrt(jnp.mean(middle * middle, -1, keepdims=True) + epsilon)
    unit_two = middle * scale_two
    normed_two = (unit_two * gain_two).astype(bf16)

    feed_out, normed_two_part, feed_grads = [], [], []
    for (first, chunk, chunks), pieces, (_, scatter) in zip(plan, feed_pieces, routes):
        out_low, part_low, *grads = feed_group(normed_two, upstream_low, pieces, chunk)
        feed_out.append(out_low)
        normed_two_part.append(part_low)
        feed_grads.append(unpack_columns(scatter(grads), chunk, chunks))
    feed_out = sum(v.astype(f32) for v in feed_out)
    normed_two_part = sum(v.astype(f32) for v in normed_two_part)
    feed_grads = [jnp.concatenate([p[j] for p in feed_grads], 1) for j in range(3)]

    feed_low = feed_out.astype(bf16).reshape(seqs, block, width)

    def own_rows(v, start):
        return lax.dynamic_slice_in_dim(v, start, half_len, 1)

    other_start = (half_len * (tp - 1) - half_start) if tp == 2 else None
    feed_other = swap_tp(own_rows(feed_low, other_start))
    feed_sum = own_rows(feed_low, half_start).astype(f32) + feed_other.astype(f32)
    block_low = (own_rows(middle.reshape(seqs, block, width), half_start) + feed_sum).astype(bf16)
    block_out = to_canonical(block_low.reshape(-1, width), order).reshape(seqs, half_len, width)

    normed_two_grad = sum_tp(normed_two_part)
    gain_two_grad = jnp.sum(normed_two_grad * unit_two, 0, keepdims=True)
    scaled_two = normed_two_grad * gain_two
    middle_grad = upstream_low.astype(f32) + scale_two * (
        scaled_two - unit_two * jnp.mean(scaled_two * unit_two, -1, keepdims=True)
    )
    branch_low = middle_grad.astype(bf16)
    mixed_grad = mm(out_full, branch_low, contract_first_last).astype(bf16)
    out_weight_grad = mm(branch_low, mixed, contract_first_last_rows).astype(bf16)

    query_grads, pack_grads = attend_back(
        counts, queries, pos, kv, keys_t, mixed, lse, mixed_grad, block
    )
    pack_sum = pack_grads[:, 0].astype(f32)
    for s in range(1, count):
        pack_sum = pack_sum + lax.ppermute(
            pack_grads[:, s], "ctx", [(i + s, i) for i in range(count - s)]
        ).astype(f32)
    pack_t = pack_sum.reshape(rows, 2 * HD).T
    grouped = jnp.concatenate([query_grads, pack_t[:HD]], 0).reshape(GROUP + 1, HD, rows)
    turned_back = rotate_rows(grouped, cosine, -sine).reshape((GROUP + 1) * HD, rows)
    projected_grad = jnp.concatenate([turned_back, pack_t[HD:]], 0).astype(bf16)
    bias_grad = jnp.sum(projected_grad.astype(f32), 1)[None]
    qkv_weight_grad = mm(normed, projected_grad, contract_first_last_rows).astype(bf16)
    attention_total = scatter_plane(
        row_pieces(jnp.concatenate([qkv_weight_grad, out_weight_grad], 1)), direct_sum
    )

    normed_one_grad = sum_tp(mm(projected_grad, qkv_full, contract_first_last))
    gain_one_grad = jnp.sum(normed_one_grad * unit_one, 0, keepdims=True)
    scaled_one = normed_one_grad * gain_one
    input_grad = middle_grad + scale_one * (
        scaled_one - unit_one * jnp.mean(scaled_one * unit_one, -1, keepdims=True)
    )
    input_grad = to_canonical(input_grad.astype(bf16), order).astype(f32)
    gain_grads = jnp.concatenate([gain_one_grad, gain_two_grad], 0)
    if order is not None:
        gain_grads = lax.dot_general(
            gain_grads, order.astype(f32), contract_last, precision=lax.Precision.HIGHEST
        )
    small = sum_all(jnp.concatenate([gain_grads.reshape(1, -1), bias_grad], 1))
    gain_total = small[:, : 2 * width].reshape(2, width)
    bias_total = small[:, 2 * width :]
    return (
        block_out,
        input_grad.reshape(seqs, block, width),
        gain_total[0],
        attention_total[:, :per_group][:, None, :],
        bias_total,
        attention_total[:, per_group:],
        gain_total[1],
        feed_grads[0],
        feed_grads[1],
        feed_grads[2],
    )


contract_first_last_rows = (((0,), (1,)), ((), ()))


def solution(mesh):
    weight = P(("fsdp", "ctx"), "tp")
    return jax.shard_map(
        shards,
        mesh=mesh,
        in_specs=(
            P("fsdp", "ctx", None),
            P("fsdp", "ctx", None),
            P("fsdp", None),
            P("fsdp", "ctx"),
            P(),
            P(("fsdp", "ctx"), "tp", None),
            P("tp", None),
            weight,
            P(),
            weight,
            weight,
            weight,
        ),
        out_specs=(
            P("fsdp", ("ctx", "tp"), None),
            P("fsdp", "ctx", None),
            P(),
            P(("fsdp", "ctx"), "tp", None),
            P("tp", None),
            weight,
            P(),
            weight,
            weight,
            weight,
        ),
        check_vma=False,
    )
```
